128 devices in a mesh: gx: 4 (over z), gy: 32 (over y, x, core).
Axes of the slice: x: 4, y: 4, z: 4, core: 2. Of those that a mesh axis runs over, the one named last changes fastest.
Arguments:
- splats: float32 [4096, 55, 128], P(('gx', 'gy')), as said below
- moment_one: float32 [4096, 55, 128], P(('gx', 'gy')), may hold values from -0.3 to 0.3
- moment_two: float32 [4096, 55, 128], P(('gx', 'gy')), may hold values from 0.001 to 1
- target: float32 [2048, 3, 256], P(('gx', 'gy')), may hold values from 0 to 1
- tile_place: int32 [2048], P(('gx', 'gy')), may hold values from 0 to 2047, as said below
- pairs: int32 [2048, 8], P(('gx', 'gy')), may hold values from -1 to 255, as said below
- fetch: int32 [128, 128, 2], P(('gx', 'gy')), may hold values from -1 to 31, as said below
Outputs:
- image: float32 [2048, 3, 256], P(('gx', 'gy'))
- splat_grad: float32 [4096, 55, 128], P(('gx', 'gy'))
- adam_step: float32 [4096, 55, 128], P(('gx', 'gy'))
The draws below stay inside these ranges and needn't reach their ends.
Inputs may be any that keep to these rules, and one draw needn't show every extreme that they name: fetch[d, o] lists up to 2 distinct blocks of owner o (indices among the owner's 32 blocks, owner o holding global blocks o * 32 to o * 32 + 31) that device d fetches; -1 marks an empty place; every device fetches 2 blocks from some owner. pairs[r] names distinct fetched places s = o * 2 + i of the device that holds row r, each with fetch[that device, o, i] >= 0; -1 marks empty places, which come last; on every device some row has all 8 places live. `tile_place`: a permutation of the view tiles; view tiles are numbered row by row, 16 to a row. z = splats[:, 2] lies between 2 and 12.
All inputs are finite; a program needn't handle non-finite values.
Results may differ from the reference program's by a relative error of at most 0.0003.
Values sent between devices are 32-bit elements; how exact they have to be, the bound alone decides.
No kernel may reach another device: no remote copies, remote signals or barrier semaphores. Data moves between devices by JAX's collectives and lax.ppermute only.
A program may use at most 128 MiB of HBM per device.

```python
import math
import jax
import jax.numpy as jnp
from jax import lax

NP = 55
BS = 128
CAP = 2
DEPTH = 8
TILES_DEV = 16
TX = 16
BLK_DEV = 32
BLOCKS = 4096
TILES = 2048
N_GX = 4
N_GY = 32


def layout(key):
    devices = N_GX * N_GY
    classes = TILES_DEV
    members = devices // TILES_DEV
    band_rows = devices // TX
    slots = devices * CAP
    keys = jax.random.split(jax.random.fold_in(key, 7), 6)
    index = jnp.arange(devices, dtype=jnp.int32)
    band_index = jnp.arange(classes, dtype=jnp.int32)
    corner_score = jax.random.randint(keys[0], (classes, devices), 0, 1 << 16) * devices + index[None, :]
    corner_owner = jnp.argsort(corner_score, axis=1).astype(jnp.int32)
    owner_corner = jnp.argsort(corner_owner, axis=1).astype(jnp.int32)
    local_score = jax.random.randint(keys[1], (devices, BLK_DEV), 0, 1 << 16) * BLK_DEV + jnp.arange(BLK_DEV, dtype=jnp.int32)[None, :]
    local_order = jnp.argsort(local_score, axis=1).astype(jnp.int32)
    local_rank = jnp.argsort(local_order, axis=1).astype(jnp.int32)
    tile_row = index // TX
    tile_col = index % TX
    inner = (tile_row >= 1) & (tile_col >= 1)
    first_score = jax.random.randint(keys[2], (classes, devices), 0, 1 << 16) * devices + index[None, :] + jnp.where(inner, 0, 1 << 24)[None, :]
    first_rank = jnp.argsort(jnp.argsort(first_score, axis=1), axis=1)
    later = jax.random.randint(keys[3], (classes, devices), 0, 1 << 16) * devices + index[None, :]
    second_score = jnp.where(first_rank < members, first_rank, members + later)
    order = jnp.argsort(second_score, axis=1).astype(jnp.int32)
    group_member = jnp.arange(members, dtype=jnp.int32)
    turn = jnp.arange(TILES_DEV, dtype=jnp.int32)
    position = jnp.where(turn[None, :] == 0, group_member[:, None], members + group_member[:, None] * (TILES_DEV - 1) + turn[None, :] - 1).reshape(-1)
    band_tiles = order[:, position]
    tile_place = (band_index[:, None] * devices + band_tiles).reshape(-1).astype(jnp.int32)
    corner_table = jnp.stack([jnp.where(inner, (tile_row - 1) * TX + tile_col - 1, -1), jnp.where(tile_row >= 1, (tile_row - 1) * TX + tile_col, -1), jnp.where(tile_col >= 1, tile_row * TX + tile_col - 1, -1), index], axis=1)
    first_corners = corner_table[order[:, :members]].reshape(classes, members * 4)
    hit_first = jnp.any(first_corners[:, :, None] == index[None, None, :], axis=1)
    full = (jax.random.randint(keys[4], (classes, devices), 0, 100) < 80) | hit_first
    live_block = (jnp.arange(CAP)[None, None, :] == 0) | full[:, :, None]
    row_corners = corner_table[band_tiles]
    device_corners = row_corners.reshape(classes, members, TILES_DEV * 4)
    need = jnp.any(device_corners[:, :, :, None] == index[None, None, None, :], axis=2)
    need_owner = jnp.take_along_axis(need, jnp.broadcast_to(owner_corner[:, None, :], need.shape), axis=2)
    live_owner = jnp.take_along_axis(live_block, jnp.broadcast_to(owner_corner[:, :, None], (classes, devices, CAP)), axis=1)
    chosen = local_order[index[None, :, None], band_index[:, None, None] * CAP + jnp.arange(CAP, dtype=jnp.int32)[None, None, :]]
    fetch = jnp.where(need_owner[:, :, :, None] & live_owner[:, None, :, :], chosen[:, None, :, :], -1)
    fetch = fetch.reshape(devices, devices, CAP).astype(jnp.int32)
    valid = row_corners >= 0
    safe = jnp.maximum(row_corners, 0)
    entry = (safe[:, :, :, None] * CAP + jnp.arange(CAP)[None, None, None, :]).reshape(classes, devices * 4 * CAP)
    entry_live = jnp.take_along_axis(live_block.reshape(classes, slots), entry, axis=1).reshape(classes, devices, 4 * CAP)
    entry_live = entry_live & jnp.repeat(valid, CAP, axis=2)
    owners = jnp.take_along_axis(corner_owner, safe.reshape(classes, -1), axis=1).reshape(classes, devices, 4)
    places = (owners[:, :, :, None] * CAP + jnp.arange(CAP)[None, None, None, :]).reshape(classes, devices, 4 * CAP)
    depth_key = jax.random.randint(keys[5], (classes, slots), 0, 1 << 12) * slots + jnp.arange(slots)[None, :]
    entry_sort_key = jnp.take_along_axis(depth_key, entry, axis=1).reshape(classes, devices, 4 * CAP)
    spare = jnp.arange(4 * CAP)[None, None, :]
    score = jnp.where(entry_live, (1 << 30) - entry_sort_key, -1 - spare)
    best, taken = lax.top_k(score, DEPTH)
    picked = jnp.take_along_axis(places, taken, axis=2)
    pairs = jnp.where(best >= 0, picked, -1).reshape(TILES, DEPTH).astype(jnp.int32)
    block_owner = jnp.repeat(index, BLK_DEV)
    block_local = jnp.tile(jnp.arange(BLK_DEV, dtype=jnp.int32), devices)
    rank = local_rank[block_owner, block_local]
    band = rank // CAP
    which = rank % CAP
    corner = owner_corner[band, block_owner]
    centre_x = (16 * (corner % TX + 1)).astype(jnp.float32)
    centre_y = (16 * (band * band_rows + corner // TX + 1)).astype(jnp.float32)
    near = 2.0 + 9.0 * depth_key[band, corner * CAP + which].astype(jnp.float32) / float((1 << 12) * slots)
    return (fetch, pairs, tile_place, centre_x, centre_y, near)


def draw_fetch(key, part):
    return layout(key)[0]


def draw_pairs(key, part):
    return layout(key)[1]


def draw_tile_place(key, part):
    return layout(key)[2]


def draw_splats(key, part):
    _, _, _, centre_x, centre_y, near = layout(key)
    keys = jax.random.split(jax.random.fold_in(key, 11), 8)
    shape = (BLOCKS, BS)
    width = 16.0 * TX
    height = 16.0 * (TILES // TX)
    harmonic_scale = jnp.where(jnp.arange(48) % 16 == 0, 0.6, 0.2)[None, :, None]
    power_draw = jax.random.uniform(keys[3], shape, jnp.float32)
    spread = 4.0
    lower, upper = (3.5, 11.0)
    logit = -8.0 + 9.0 * power_draw ** 20
    jitter = 0.9
    coeffs = jax.random.normal(keys[4], (BLOCKS, 48, BS), jnp.float32) * harmonic_scale
    across = centre_x[:, None] + jax.random.uniform(keys[0], shape, jnp.float32, -spread, spread)
    down = centre_y[:, None] + jax.random.uniform(keys[1], shape, jnp.float32, -spread, spread)
    depth = near[:, None] + jax.random.uniform(keys[2], shape, jnp.float32, 0.0, jitter)
    first_scale = jax.random.uniform(keys[5], shape, jnp.float32, math.log(lower), math.log(upper))
    second_scale = jax.random.uniform(keys[6], shape, jnp.float32, math.log(lower), math.log(upper))
    angle = jax.random.uniform(keys[7], shape, jnp.float32, -math.pi, math.pi)
    place_x = (across - 0.5 * width) * depth / width
    place_y = (down - 0.5 * height) * depth / width
    head = jnp.stack([place_x, place_y, depth, first_scale, second_scale, angle, logit], axis=1)
    return jnp.concatenate([head, coeffs], axis=1).astype(jnp.float32)


def levels(key, dims, cuts, least, high):
    factor_of = 1.0
    for dim, parts in cuts:
        heights = jax.random.uniform(jax.random.fold_in(jax.random.fold_in(key, 6), dim), (parts,), jnp.float32, least / len(cuts), high / len(cuts))
        factor_of = factor_of * jnp.repeat(jnp.exp(heights), dims[dim] // parts).reshape((-1,) + (1,) * (len(dims) - 1 - dim))
    return factor_of


def noise(own_key, shape, scale, limit, cuts=(), held_as=jnp.bfloat16):
    result = jax.random.normal(own_key, shape, jnp.float32) * scale
    if len(cuts) > 0:
        result = levels(own_key, shape, cuts, -0.22, 0.18) * result
    return jnp.clip(result, min=-limit, max=limit).astype(held_as)


def setup_inputs(seed: int = 0) -> dict:
    streams_of = jax.random.split(jax.random.key(seed), 8)
    splats = draw_splats(jax.random.fold_in(streams_of[7], 71), 0)
    moment_one = noise(streams_of[1], (BLOCKS, NP, BS), 0.05, 0.3, ((0, 128),), jnp.float32)
    moment_two = jnp.clip(jnp.exp(math.log(1.0) - 6.9077552 * jax.random.uniform(streams_of[2], (BLOCKS, NP, BS), jnp.float32) ** levels(streams_of[2], (BLOCKS, NP, BS), ((0, 128),), -0.2, 0.2)), 0.001, 1.0)
    target = jnp.clip(1.0 * jax.random.uniform(streams_of[3], (TILES, 3, 256), jnp.float32) ** levels(streams_of[3], (TILES, 3, 256), ((0, 128),), -0.2, 0.2), 0.0, 1.0)
    tile_place = draw_tile_place(jax.random.fold_in(streams_of[7], 71), 0)
    pairs = draw_pairs(jax.random.fold_in(streams_of[7], 71), 0)
    fetch = draw_fetch(jax.random.fold_in(streams_of[7], 71), 0)
    return dict(splats=splats, moment_one=moment_one, moment_two=moment_two, target=target, tile_place=tile_place, pairs=pairs, fetch=fetch)


HARMONIC_ZERO = 0.28209479177387814
HARMONIC_ONE = 0.4886025119029199
HARMONIC_TWO = (1.0925484305920792, -1.0925484305920792, 0.31539156525252005, -1.0925484305920792, 0.5462742152960396)
HARMONIC_THREE = (-0.5900435899266435, 2.890611442640554, -0.4570457994644658, 0.3731763325901154, -0.4570457994644658, 1.445305721320277, -0.5900435899266435)

def harmonics(east, north, ahead):
    east_east = east * east
    north_north = north * north
    ahead_ahead = ahead * ahead
    terms = [jnp.full_like(east, HARMONIC_ZERO), -HARMONIC_ONE * north, HARMONIC_ONE * ahead, -HARMONIC_ONE * east, HARMONIC_TWO[0] * east * north, HARMONIC_TWO[1] * north * ahead, HARMONIC_TWO[2] * (2.0 * ahead_ahead - east_east - north_north), HARMONIC_TWO[3] * east * ahead, HARMONIC_TWO[4] * (east_east - north_north), HARMONIC_THREE[0] * north * (3.0 * east_east - north_north), HARMONIC_THREE[1] * east * north * ahead, HARMONIC_THREE[2] * north * (4.0 * ahead_ahead - east_east - north_north), HARMONIC_THREE[3] * ahead * (2.0 * ahead_ahead - 3.0 * east_east - 3.0 * north_north), HARMONIC_THREE[4] * east * (4.0 * ahead_ahead - east_east - north_north), HARMONIC_THREE[5] * ahead * (east_east - north_north), HARMONIC_THREE[6] * east * (east_east - 3.0 * north_north)]
    return jnp.stack(terms, axis=1)

def derive(raw, width, height):
    place_x = raw[:, 0]
    place_y = raw[:, 1]
    place_z = raw[:, 2]
    screen_u = width * place_x / place_z + 0.5 * width
    screen_v = width * place_y / place_z + 0.5 * height
    inverse_one = jnp.exp(-2.0 * raw[:, 3])
    inverse_two = jnp.exp(-2.0 * raw[:, 4])
    cosine = jnp.cos(raw[:, 5])
    sine = jnp.sin(raw[:, 5])
    conic_a = cosine * cosine * inverse_one + sine * sine * inverse_two
    conic_b = cosine * sine * (inverse_one - inverse_two)
    conic_c = sine * sine * inverse_one + cosine * cosine * inverse_two
    opacity = jax.nn.sigmoid(raw[:, 6])
    length = jnp.sqrt(place_x * place_x + place_y * place_y + place_z * place_z)
    basis = harmonics(place_x / length, place_y / length, place_z / length)
    coeffs = raw[:, 7:].reshape(raw.shape[0], 3, 16, raw.shape[2])
    colors = 0.5 + lax.optimization_barrier(jnp.sum(coeffs * basis[:, None], axis=2))
    head = jnp.stack([screen_u, screen_v, conic_a, conic_b, conic_c, opacity], axis=1)
    return jnp.concatenate([head, colors], axis=1)

def composite(screens, pixel_x, pixel_y):

    def advance(carry, screen_splat):
        log_trans, pixel_colour = carry
        delta_x = pixel_x[:, :, None] - screen_splat[:, None, 0]
        delta_y = pixel_y[:, :, None] - screen_splat[:, None, 1]
        power = -0.5 * (screen_splat[:, None, 2] * delta_x * delta_x + 2.0 * screen_splat[:, None, 3] * delta_x * delta_y + screen_splat[:, None, 4] * delta_y * delta_y)
        alpha = screen_splat[:, None, 5] * jnp.exp(power)
        log_keep = jnp.log1p(-alpha)
        before = jnp.cumsum(log_keep, axis=2) - log_keep
        blend_weight = alpha * jnp.exp(log_trans[:, :, None] + before)
        pixel_colour = pixel_colour + jnp.einsum('ylo,yeo->yel', blend_weight, screen_splat[:, 6:9], precision=lax.Precision.HIGHEST)
        return ((log_trans + lax.optimization_barrier(jnp.sum(log_keep, axis=2)), pixel_colour), None)
    count = screens.shape[0]
    start = (jnp.zeros((count, 256), jnp.float32), jnp.zeros((count, 3, 256), jnp.float32))
    (_, pixel_colour), _ = lax.scan(jax.checkpoint(advance), start, jnp.moveaxis(screens, 1, 0))
    return pixel_colour

def reference(splats, moment_one, moment_two, target, tile_place, pairs, fetch):
    devices = N_GX * N_GY
    width = 16.0 * TX
    height = 16.0 * (TILES // TX)
    screen_all, pull_all = jax.vjp(lambda raw: derive(raw, width, height), splats)
    rows = jnp.arange(TILES, dtype=jnp.int32)
    device_of = rows // TILES_DEV
    place = jnp.maximum(pairs, 0).astype(jnp.int32)
    flat_index = (device_of[:, None] * (devices * CAP) + place).astype(jnp.int32)
    local = fetch.reshape(-1)[flat_index]
    block_id = jnp.where(pairs >= 0, place // CAP * BLK_DEV + local, 0).astype(jnp.int32)
    used = (pairs >= 0).astype(jnp.float32)
    pixel = jnp.arange(256, dtype=jnp.int32)
    corner_x = (tile_place % TX * 16).astype(jnp.float32)
    corner_y = (tile_place // TX * 16).astype(jnp.float32)
    pixel_x = corner_x[:, None] + (pixel % 16).astype(jnp.float32)[None, :] + 0.5
    pixel_y = corner_y[:, None] + (pixel // 16).astype(jnp.float32)[None, :] + 0.5
    group = 16
    groups = TILES // group

    def one_group(total, pieces):
        ids, mask, across, down, goal = pieces
        slots = screen_all[ids] * mask[:, :, None, None]

        def objective(screens):
            image = composite(screens, across, down)
            residual = image - goal
            return (image, jnp.sum(residual * residual) / 512.0)
        (image, loss), pull = jax.vjp(objective, slots)
        grads, = pull((jnp.zeros_like(image), jnp.ones_like(loss)))
        grads = grads * mask[:, :, None, None]
        total = total.at[ids.reshape(-1)].add(grads.reshape((-1,) + grads.shape[2:]))
        return (total, image)
    pieces = (block_id.reshape(groups, group, DEPTH), used.reshape(groups, group, DEPTH), pixel_x.reshape(groups, group, 256), pixel_y.reshape(groups, group, 256), target.reshape(groups, group, 3, 256))
    total, images = lax.scan(one_group, jnp.zeros_like(screen_all), pieces)
    image = images.reshape(TILES, 3, 256)
    splat_grad, = pull_all(total)
    first = 0.9 * moment_one + 0.1 * splat_grad
    second_moment = 0.999 * moment_two + 0.001 * splat_grad * splat_grad
    adam_step = first / (jnp.sqrt(second_moment) + 1e-08)
    return (image, splat_grad, adam_step)
```

```python
import functools

import jax
import jax.numpy as jnp
import numpy as np
from jax import lax
from jax.experimental import pallas as pl
from jax.experimental.pallas import tpu as pltpu
from jax.sharding import PartitionSpec as P

TX = 16
BLOCK = 128
SEGMENTS = 8
STEPS = BLOCK // SEGMENTS
SLOTS = 8
PIXELS = 256
LOG2_E = 1.4426950408889634
FORM_SCALE = 0.8493218002880191
SMOOTH_TRACE = 0.75
UNROLL = 8

HARMONIC_ZERO = 0.28209479177387814
HARMONIC_ONE = 0.4886025119029199
HARMONIC_TWO = (
    1.0925484305920792,
    -1.0925484305920792,
    0.31539156525252005,
    -1.0925484305920792,
    0.5462742152960396,
)
HARMONIC_THREE = (
    -0.5900435899266435,
    2.890611442640554,
    -0.4570457994644658,
    0.3731763325901154,
    -0.4570457994644658,
    1.445305721320277,
    -0.5900435899266435,
)


def harmonics(east, north, ahead):
    east_east = east * east
    north_north = north * north
    ahead_ahead = ahead * ahead
    terms = [
        jnp.full_like(east, HARMONIC_ZERO),
        -HARMONIC_ONE * north,
        HARMONIC_ONE * ahead,
        -HARMONIC_ONE * east,
        HARMONIC_TWO[0] * east * north,
        HARMONIC_TWO[1] * north * ahead,
        HARMONIC_TWO[2] * (2.0 * ahead_ahead - east_east - north_north),
        HARMONIC_TWO[3] * east * ahead,
        HARMONIC_TWO[4] * (east_east - north_north),
        HARMONIC_THREE[0] * north * (3.0 * east_east - north_north),
        HARMONIC_THREE[1] * east * north * ahead,
        HARMONIC_THREE[2] * north * (4.0 * ahead_ahead - east_east - north_north),
        HARMONIC_THREE[3] * ahead * (2.0 * ahead_ahead - 3.0 * east_east - 3.0 * north_north),
        HARMONIC_THREE[4] * east * (4.0 * ahead_ahead - east_east - north_north),
        HARMONIC_THREE[5] * ahead * (east_east - north_north),
        HARMONIC_THREE[6] * east * (east_east - 3.0 * north_north),
    ]
    return jnp.stack(terms, axis=1)


def derive(raw, width, height):
    place_x = raw[:, 0]
    place_y = raw[:, 1]
    place_z = raw[:, 2]
    screen_u = width * place_x / place_z + 0.5 * width
    screen_v = width * place_y / place_z + 0.5 * height
    inverse_one = jnp.exp(-2.0 * raw[:, 3])
    inverse_two = jnp.exp(-2.0 * raw[:, 4])
    cosine = jnp.cos(raw[:, 5])
    sine = jnp.sin(raw[:, 5])
    conic_a = cosine * cosine * inverse_one + sine * sine * inverse_two
    conic_b = cosine * sine * (inverse_one - inverse_two)
    conic_c = sine * sine * inverse_one + cosine * cosine * inverse_two
    log_opacity = jax.nn.log_sigmoid(raw[:, 6])
    length = jnp.sqrt(place_x * place_x + place_y * place_y + place_z * place_z)
    basis = harmonics(place_x / length, place_y / length, place_z / length)
    coeffs = raw[:, 7:].reshape(raw.shape[0], 3, 16, raw.shape[2])
    colors = 0.5 + jnp.sum(coeffs * basis[:, None], axis=2)
    head = jnp.stack([screen_u, screen_v, conic_a, conic_b, conic_c, log_opacity], axis=1)
    return jnp.concatenate([head, colors], axis=1)


def lane_order():
    order = np.zeros((BLOCK, BLOCK), np.float32)
    for step in range(STEPS):
        for segment in range(SEGMENTS):
            order[STEPS * segment + step, SEGMENTS * step + segment] = 1.0
    return order


def pixel_tables():
    pixel = np.arange(PIXELS)
    across = (pixel % 16) - 7.5
    down = (pixel // 16) - 7.5
    ones = np.ones(PIXELS)
    moments = np.zeros((8, PIXELS), np.float32)
    moments[0:6] = [ones, across, down, across * across, across * down, down * down]
    quadratic = np.zeros((32, PIXELS), np.float32)
    for base in range(6):
        quadratic[3 * base : 3 * base + 3] = moments[base]
    forms = np.zeros((32, 3 * PIXELS), np.float32)
    forms[0:3, :PIXELS] = across
    forms[3:6, :PIXELS] = down
    forms[6:9, :PIXELS] = ones
    forms[9:12, PIXELS : 2 * PIXELS] = down
    forms[12:15, PIXELS : 2 * PIXELS] = ones
    forms[15:18, 2 * PIXELS :] = ones
    return quadratic, forms, moments


def rounded(value):
    return value.astype(jnp.bfloat16).astype(jnp.float32)


def split3(value):
    high = rounded(value)
    rest = value - high
    middle = rounded(rest)
    return high, middle, rest - middle


def split2(value):
    high = rounded(value)
    return high, rounded(value - high)


CONTRACT_ROWS = (((0,), (0,)), ((), ()))
CONTRACT_LANES = (((1,), (1,)), ((), ()))


def blend_kernel(
    pairs_ref, place_ref, arrived_ref, target_ref, quadratic_ref, forms_ref, moments_ref,
    image_ref, grad_ref,
    block_ref, form_ref, tint_ref, power_ref, alpha_ref, weight_ref, trans_ref, local_ref,
    carry_ref, behind_ref, glow_ref, rows_ref, split_ref, sums_ref,
):
    f32 = jnp.float32
    bf16 = jnp.bfloat16
    tiles = target_ref.shape[0]
    segment = lax.broadcasted_iota(jnp.int32, (SEGMENTS, PIXELS), 0)
    slot_row = lax.broadcasted_iota(jnp.int32, (SLOTS, BLOCK), 0)
    lane_segment = lax.rem(lax.broadcasted_iota(jnp.int32, (SEGMENTS, BLOCK), 1), SEGMENTS)
    own_segment = (lane_segment == lax.broadcasted_iota(jnp.int32, (SEGMENTS, BLOCK), 0)).astype(f32)

    def clear(place, steep):
        grad_ref[place] = jnp.zeros(grad_ref.shape[1:], f32)
        head = arrived_ref[place, 0:8, :]
        return jnp.maximum(steep, head * head)

    steep = lax.fori_loop(0, grad_ref.shape[0], clear, jnp.zeros((8, BLOCK), f32), unroll=8)
    smooth = jnp.max(steep[2:3] + steep[3:4] + steep[4:5]) <= SMOOTH_TRACE
    form_ref[...] = jnp.zeros_like(form_ref)
    tint_ref[...] = jnp.zeros_like(tint_ref)
    rows_ref[...] = jnp.zeros_like(rows_ref)
    rows_ref[0:8, :] = moments_ref[...]
    glow_ref[...] = jnp.zeros_like(glow_ref)

    def tile(row, quick, unroll):
        view = place_ref[row]
        center_x = (16 * lax.rem(view, TX) + 8).astype(f32)
        center_y = (16 * lax.div(view, TX) + 8).astype(f32)
        live = jnp.zeros((SLOTS, BLOCK), f32)
        places = []
        for slot in range(SLOTS):
            place = pairs_ref[row, slot]
            live = jnp.where(slot_row == slot, (place >= 0).astype(f32), live)
            place = jnp.maximum(place, 0)
            places.append(place)
            block_ref[16 * slot : 16 * slot + 9, :] = arrived_ref[place]

        def fetched(base):
            return block_ref[pl.ds(base, SLOTS, stride=16), :]

        across = fetched(0) - center_x
        down = fetched(1) - center_y
        form_xx, form_xy, form_yy = fetched(2), fetched(3), fetched(4)
        log_opacity = jnp.where(live > 0.0, fetched(5), -1e9)
        shift_one = -(form_xx * across + form_xy * down)
        shift_two = -(form_yy * down)
        if quick:
            shift_one = jnp.clip(shift_one, -1e4, 1e4)
            shift_two = jnp.clip(shift_two, -1e4, 1e4)
            values = (
                log_opacity - shift_one * shift_one - shift_two * shift_two,
                -2.0 * (form_xx * shift_one),
                -2.0 * (form_xy * shift_one + form_yy * shift_two),
                -(form_xx * form_xx),
                -2.0 * (form_xx * form_xy),
                -(form_xy * form_xy + form_yy * form_yy),
            )
        else:
            values = (form_xx, form_xy, shift_one, form_yy, shift_two, log_opacity)
        for base, value in enumerate(values):
            for part, piece in enumerate(split3(value)):
                form_ref[pl.ds(8 * (3 * base + part), SLOTS), :] = piece
        for channel in range(3):
            high, low = split2(fetched(6 + channel))
            for base, piece in enumerate((high, low, high)):
                tint_ref[pl.ds(8 * (3 * base + channel), SLOTS), :] = piece

        def ahead(first):
            chains = [(inner, half) for inner in range(unroll) for half in range(2)]
            for inner in range(unroll):
                lhs = form_ref[pl.ds(first + inner, 32, stride=8), :].astype(bf16)
                rhs = quadratic_ref if quick else forms_ref
                power_ref[inner, :, 0 : rhs.shape[1]] = lax.dot_general(
                    lhs, rhs[...], CONTRACT_ROWS, preferred_element_type=f32
                )
            trans = [jnp.ones((SEGMENTS, 128), f32) for _ in chains]
            for pair in range(STEPS // 2):
                weights = [[] for _ in chains]
                for step in (2 * pair, 2 * pair + 1):
                    eight = slice(8 * step, 8 * step + 8)
                    for chain, (inner, half) in enumerate(chains):
                        lanes = slice(128 * half, 128 * half + 128)
                        if quick:
                            exponent = jnp.minimum(power_ref[inner, eight, lanes], 0.0)
                        else:
                            one = power_ref[inner, eight, lanes]
                            two = power_ref[inner, eight, 256 + 128 * half : 384 + 128 * half]
                            three = power_ref[inner, eight, 512 + 128 * half : 640 + 128 * half]
                            exponent = three - one * one - two * two
                        alpha = jnp.exp2(exponent)
                        weight = alpha * trans[chain]
                        trans[chain] = trans[chain] - weight
                        alpha_ref[first + inner, eight, lanes] = alpha
                        weight_ref[first + inner, eight, lanes] = weight
                        weights[chain].append(weight)
                for chain, (inner, half) in enumerate(chains):
                    lanes = slice(128 * half, 128 * half + 128)
                    value = jnp.concatenate(weights[chain], axis=0)
                    high = value.astype(bf16)
                    split_ref[inner, 16 * pair : 16 * pair + 16, lanes] = high
                    split_ref[inner, 128 + 16 * pair : 144 + 16 * pair, lanes] = (
                        value - high.astype(f32)
                    ).astype(bf16)
            for chain, (inner, half) in enumerate(chains):
                trans_ref[first + inner, :, 128 * half : 128 * half + 128] = trans[chain]
            for inner in range(unroll):
                parts = [
                    own_segment * tint_ref[pl.ds(8 * base + first + inner, 1), :] for base in range(6)
                ]
                lhs = jnp.concatenate(parts, axis=0).astype(bf16)
                found = lax.dot_general(
                    jnp.concatenate([lhs, lhs], axis=1), split_ref[inner, 0 : 2 * BLOCK, :],
                    (((1,), (0,)), ((), ())), preferred_element_type=f32,
                )
                local_ref[first + inner] = found[0:24] + found[24:48]

        if unroll == SLOTS:
            ahead(0)
        else:
            lax.fori_loop(0, SLOTS // unroll, lambda group, _: (ahead(group * unroll), 0)[1], 0)

        before = jnp.ones((1, PIXELS), f32)
        seen = [jnp.zeros((SEGMENTS, PIXELS), f32) for _ in range(3)]
        for slot in range(SLOTS):
            through = trans_ref[slot]
            for reach in (1, 2, 4):
                through = through * jnp.where(segment >= reach, pltpu.roll(through, reach, 0), 1.0)
            carry = jnp.where(segment >= 1, pltpu.roll(through, 1, 0), 1.0) * before
            carry_ref[slot] = carry
            for channel in range(3):
                seen[channel] = seen[channel] + carry * local_ref[slot, 8 * channel : 8 * channel + 8, :]
            before = before * through[7:8]
        glow = []
        for channel in range(3):
            color = jnp.sum(seen[channel], axis=0, keepdims=True)
            image_ref[row, channel : channel + 1, :] = color
            value = (color - target_ref[row, channel : channel + 1, :]) * (2.0 / 512.0)
            glow.append(value)
            high, low = split2(value)
            for base, piece in enumerate((high, high, low)):
                glow_ref[3 * base + channel : 3 * base + channel + 1, :] = piece
            rows_ref[8 + channel : 9 + channel, :] = high
            rows_ref[16 + channel : 17 + channel, :] = low

        after = jnp.zeros((1, PIXELS), f32)
        for slot in reversed(range(SLOTS)):
            through = trans_ref[slot]
            light = (
                local_ref[slot, 0:8, :] * glow[0]
                + local_ref[slot, 8:16, :] * glow[1]
                + local_ref[slot, 16:24, :] * glow[2]
            )
            for reach in (1, 2, 4):
                inside = segment < SEGMENTS - reach
                light = light + through * jnp.where(inside, pltpu.roll(light, SEGMENTS - reach, 0), 0.0)
                through = through * jnp.where(inside, pltpu.roll(through, SEGMENTS - reach, 0), 1.0)
            start = light + through * after
            behind_ref[slot] = jnp.where(segment < SEGMENTS - 1, pltpu.roll(start, SEGMENTS - 1, 0), after)
            after = start[0:1]

        glow_parts = glow_ref[...].astype(bf16)
        lhs_rows = rows_ref[...].astype(bf16)

        def back(first):
            chains = [(inner, half) for inner in range(unroll) for half in range(2)]
            for inner in range(unroll):
                power_ref[inner, :, 0:PIXELS] = lax.dot_general(
                    tint_ref[pl.ds(first + inner, 16, stride=8), :].astype(bf16), glow_parts,
                    CONTRACT_ROWS, preferred_element_type=f32,
                )
            behind = [
                behind_ref[first + inner, :, 128 * half : 128 * half + 128] for inner, half in chains
            ]
            for pair in reversed(range(STEPS // 2)):
                pulls = [[] for _ in chains]
                weights = [[] for _ in chains]
                for step in (2 * pair + 1, 2 * pair):
                    eight = slice(8 * step, 8 * step + 8)
                    for chain, (inner, half) in enumerate(chains):
                        lanes = slice(128 * half, 128 * half + 128)
                        alpha = alpha_ref[first + inner, eight, lanes]
                        carry = carry_ref[first + inner, :, lanes]
                        weight = weight_ref[first + inner, eight, lanes] * carry
                        gain = power_ref[inner, eight, lanes] - behind[chain]
                        behind[chain] = behind[chain] + alpha * gain
                        pulls[chain].append(weight * gain)
                        weights[chain].append(weight)
                for chain, (inner, half) in enumerate(chains):
                    lanes = slice(128 * half, 128 * half + 128)
                    for base, parts in ((0, pulls[chain]), (256, weights[chain])):
                        value = jnp.concatenate([parts[1], parts[0]], axis=0)
                        high = value.astype(bf16)
                        low = (value - high.astype(f32)).astype(bf16)
                        split_ref[inner, base + 16 * pair : base + 16 * pair + 16, lanes] = high
                        split_ref[inner, base + 128 + 16 * pair : base + 144 + 16 * pair, lanes] = low
            for inner in range(unroll):
                found = lax.dot_general(
                    lhs_rows, split_ref[inner], CONTRACT_LANES, preferred_element_type=f32
                )
                tints = found[8:24, 256:384] + found[8:24, 384:512]
                sums_ref[pl.ds(16 * (first + inner), 8), :] = found[0:8, 0:128] + found[0:8, 128:256]
                sums_ref[pl.ds(16 * (first + inner) + 8, 8), :] = tints[0:8] + tints[8:16]

        if unroll == SLOTS:
            back(0)
        else:
            lax.fori_loop(0, SLOTS // unroll, lambda group, _: (back(group * unroll), 0)[1], 0)

        def summed(base):
            return sums_ref[pl.ds(base, SLOTS, stride=16), :]

        total, sum_x, sum_y = summed(0), summed(1), summed(2)
        off_x = sum_x - across * total
        off_y = sum_y - down * total
        sum_xx = summed(3) - across * (sum_x + off_x)
        sum_xy = summed(4) - across * sum_y - down * off_x
        sum_yy = summed(5) - down * (sum_y + off_y)
        values = (off_x, off_y, sum_xx, sum_xy, sum_yy, total, summed(8), summed(9), summed(10))
        for base, value in enumerate(values):
            block_ref[pl.ds(base, SLOTS, stride=16), :] = value
        for slot in range(SLOTS):
            grad_ref[places[slot]] = grad_ref[places[slot]] + block_ref[16 * slot : 16 * slot + 9, :]

    @pl.when(smooth)
    def _():
        lax.fori_loop(0, tiles, lambda row, _: (tile(row, True, UNROLL), 0)[1], 0)

    @pl.when(jnp.logical_not(smooth))
    def _():
        lax.fori_loop(0, tiles, lambda row, _: (tile(row, False, 1), 0)[1], 0)


def blend(pairs, tile_place, arrived, target):
    quadratic, forms, moments = pixel_tables()
    tiles = target.shape[0]
    f32 = jnp.float32
    vmem = pl.BlockSpec(memory_space=pltpu.VMEM)
    smem = pl.BlockSpec(memory_space=pltpu.SMEM)
    return pl.pallas_call(
        blend_kernel,
        out_shape=(
            jax.ShapeDtypeStruct((tiles, 3, PIXELS), f32),
            jax.ShapeDtypeStruct(arrived.shape, f32),
        ),
        in_specs=[smem, smem, vmem, vmem, vmem, vmem, vmem],
        out_specs=(vmem, vmem),
        scratch_shapes=[
            pltpu.VMEM((SLOTS * 16, BLOCK), f32),
            pltpu.VMEM((32 * SLOTS, BLOCK), f32),
            pltpu.VMEM((16 * SLOTS, BLOCK), f32),
            pltpu.VMEM((UNROLL, BLOCK, 3 * PIXELS), f32),
            pltpu.VMEM((SLOTS, BLOCK, PIXELS), f32),
            pltpu.VMEM((SLOTS, BLOCK, PIXELS), f32),
            pltpu.VMEM((SLOTS, SEGMENTS, PIXELS), f32),
            pltpu.VMEM((SLOTS, 3 * SEGMENTS, PIXELS), f32),
            pltpu.VMEM((SLOTS, SEGMENTS, PIXELS), f32),
            pltpu.VMEM((SLOTS, SEGMENTS, PIXELS), f32),
            pltpu.VMEM((16, PIXELS), f32),
            pltpu.VMEM((32, PIXELS), f32),
            pltpu.VMEM((UNROLL, 4 * BLOCK, PIXELS), jnp.bfloat16),
            pltpu.VMEM((SLOTS * 16, BLOCK), f32),
        ],
        compiler_params=pltpu.CompilerParams(vmem_limit_bytes=48 << 20),
        cost_estimate=pl.CostEstimate(flops=200_000_000, bytes_accessed=6_000_000, transcendentals=4_000_000),
        name="blend",
    )(
        pairs, tile_place, arrived, target, jnp.asarray(quadratic, jnp.bfloat16),
        jnp.asarray(forms, jnp.bfloat16), jnp.asarray(moments, f32),
    )


def sent_rows(raw, width, height):
    found, pull = jax.vjp(functools.partial(derive, width=width, height=height), raw)
    conic_a, conic_b, conic_c = found[:, 2], found[:, 3], found[:, 4]
    steep = conic_a > 1e-30
    over = lax.rsqrt(jnp.where(steep, conic_a, 1.0))
    form_xx = jnp.sqrt(conic_a)
    form_xy = jnp.where(steep, conic_b * over, 0.0)
    form_yy = jnp.where(steep, jnp.exp(-raw[:, 3] - raw[:, 4]) * over, jnp.sqrt(conic_c))
    rows = jnp.stack(
        [found[:, 0], found[:, 1], FORM_SCALE * form_xx, FORM_SCALE * form_xy, FORM_SCALE * form_yy,
         LOG2_E * found[:, 5]], axis=1)
    rows = jnp.concatenate([rows, found[:, 6:9]], axis=1)
    rows = jnp.einsum("brl,lm->brm", rows, jnp.asarray(lane_order()), precision=lax.Precision.HIGHEST)
    return rows, (conic_a, conic_b, conic_c), pull


def trade(payload):
    return lax.all_to_all(payload, ("gx", "gy"), split_axis=0, concat_axis=0, tiled=True)


def local(splats, moment_one, moment_two, target, tile_place, pairs, fetch):
    devices = lax.axis_size("gx") * lax.axis_size("gy")
    tiles_here = target.shape[0]
    width = 16.0 * TX
    height = 16.0 * (tiles_here * devices // TX)
    asked = lax.all_to_all(fetch[0], ("gx", "gy"), split_axis=0, concat_axis=0, tiled=True)
    wanted = jnp.maximum(asked, 0)
    own_rows, (conic_a, conic_b, conic_c), pull = sent_rows(splats, width, height)
    payload = own_rows[wanted]
    arrived = trade(payload)
    arrived = arrived.reshape((-1,) + payload.shape[2:])
    image, received = blend(pairs, tile_place, arrived, target)
    returned = trade(received.reshape(payload.shape))
    owner_pick = (asked.reshape(-1)[None, :] == jnp.arange(splats.shape[0])[:, None]).astype(jnp.float32)
    summed = jnp.dot(
        owner_pick, returned.reshape(owner_pick.shape[1], -1), precision=lax.Precision.HIGHEST
    )
    summed = summed.reshape((splats.shape[0],) + returned.shape[2:])
    summed = jnp.einsum("brm,lm->brl", summed, jnp.asarray(lane_order()), precision=lax.Precision.HIGHEST)
    off_x, off_y = summed[:, 0], summed[:, 1]
    pulled = jnp.stack(
        [conic_a * off_x + conic_b * off_y, conic_b * off_x + conic_c * off_y,
         -0.5 * summed[:, 2], -summed[:, 3], -0.5 * summed[:, 4], summed[:, 5]], axis=1)
    (splat_grad,) = pull(jnp.concatenate([pulled, summed[:, 6:9]], axis=1))
    first = 0.9 * moment_one + 0.1 * splat_grad
    second_moment = 0.999 * moment_two + 0.001 * splat_grad * splat_grad
    adam_step = first / (jnp.sqrt(second_moment) + 1e-08)
    return (image, splat_grad, adam_step)


def solution(mesh):
    return jax.shard_map(
        local,
        mesh=mesh,
        in_specs=(
            P(("gx", "gy"), None, None),
            P(("gx", "gy"), None, None),
            P(("gx", "gy"), None, None),
            P(("gx", "gy"), None, None),
            P(("gx", "gy")),
            P(("gx", "gy"), None),
            P(("gx", "gy"), None, None),
        ),
        out_specs=(
            P(("gx", "gy"), None, None),
            P(("gx", "gy"), None, None),
            P(("gx", "gy"), None, None),
        ),
        check_vma=False,
    )
```

```python
import functools

import jax
import jax.numpy as jnp
import numpy as np
from jax import lax
from jax.experimental import pallas as pl
from jax.experimental.pallas import tpu as pltpu
from jax.sharding import PartitionSpec as P

TX = 16
BLOCK = 128
SEGMENTS = 8
STEPS = BLOCK // SEGMENTS
SLOTS = 8
PIXELS = 256
LOG2_E = 1.4426950408889634
FORM_SCALE = 0.8493218002880191
SMOOTH_TRACE = 0.75
GROUP = 2

HARMONIC_ZERO = 0.28209479177387814
HARMONIC_ONE = 0.4886025119029199
HARMONIC_TWO = (
    1.0925484305920792,
    -1.0925484305920792,
    0.31539156525252005,
    -1.0925484305920792,
    0.5462742152960396,
)
HARMONIC_THREE = (
    -0.5900435899266435,
    2.890611442640554,
    -0.4570457994644658,
    0.3731763325901154,
    -0.4570457994644658,
    1.445305721320277,
    -0.5900435899266435,
)


def harmonics(east, north, ahead):
    east_east = east * east
    north_north = north * north
    ahead_ahead = ahead * ahead
    terms = [
        jnp.full_like(east, HARMONIC_ZERO),
        -HARMONIC_ONE * north,
        HARMONIC_ONE * ahead,
        -HARMONIC_ONE * east,
        HARMONIC_TWO[0] * east * north,
        HARMONIC_TWO[1] * north * ahead,
        HARMONIC_TWO[2] * (2.0 * ahead_ahead - east_east - north_north),
        HARMONIC_TWO[3] * east * ahead,
        HARMONIC_TWO[4] * (east_east - north_north),
        HARMONIC_THREE[0] * north * (3.0 * east_east - north_north),
        HARMONIC_THREE[1] * east * north * ahead,
        HARMONIC_THREE[2] * north * (4.0 * ahead_ahead - east_east - north_north),
        HARMONIC_THREE[3] * ahead * (2.0 * ahead_ahead - 3.0 * east_east - 3.0 * north_north),
        HARMONIC_THREE[4] * east * (4.0 * ahead_ahead - east_east - north_north),
        HARMONIC_THREE[5] * ahead * (east_east - north_north),
        HARMONIC_THREE[6] * east * (east_east - 3.0 * north_north),
    ]
    return terms


def lane_order():
    order = np.zeros((BLOCK, BLOCK), np.float32)
    for step in range(STEPS):
        for segment in range(SEGMENTS):
            order[STEPS * segment + step, SEGMENTS * step + segment] = 1.0
    return order


def pixel_tables():
    pixel = np.arange(PIXELS)
    across = (pixel % 16) - 7.5
    down = (pixel // 16) - 7.5
    ones = np.ones(PIXELS)
    moments = np.zeros((8, PIXELS), np.float32)
    moments[0:6] = [ones, across, down, across * across, across * down, down * down]
    quadratic = np.zeros((32, PIXELS), np.float32)
    for base in range(6):
        quadratic[3 * base : 3 * base + 3] = moments[base]
    forms = np.zeros((32, 3 * PIXELS), np.float32)
    forms[0:3, :PIXELS] = across
    forms[3:6, :PIXELS] = down
    forms[6:9, :PIXELS] = ones
    forms[9:12, PIXELS : 2 * PIXELS] = down
    forms[12:15, PIXELS : 2 * PIXELS] = ones
    forms[15:18, 2 * PIXELS :] = ones
    return quadratic, forms, moments


def rounded(value):
    return value.astype(jnp.bfloat16).astype(jnp.float32)


def split3(value):
    high = rounded(value)
    rest = value - high
    middle = rounded(rest)
    return high, middle, rest - middle


def split2(value):
    high = rounded(value)
    return high, rounded(value - high)


CONTRACT_ROWS = (((0,), (0,)), ((), ()))
CONTRACT_LANES = (((1,), (1,)), ((), ()))


def blend_kernel(
    pairs_ref, place_ref, arrived_ref, target_ref, quadratic_ref, forms_ref, moments_ref,
    image_ref, grad_ref,
    block_ref, form_ref, tint_ref, center_ref, steep_ref, power_ref, glow_power_ref,
    alpha_ref, weight_ref, trans_ref, local_ref, carry_ref, behind_ref, glow_ref, rows_ref,
    sums_ref,
):
    f32 = jnp.float32
    bf16 = jnp.bfloat16
    tiles = target_ref.shape[1]
    segment = lax.broadcasted_iota(jnp.int32, (SEGMENTS, PIXELS), 0)
    slot_row = lax.broadcasted_iota(jnp.int32, (SLOTS, BLOCK), 0)
    lane_segment = lax.rem(lax.broadcasted_iota(jnp.int32, (SEGMENTS, BLOCK), 1), SEGMENTS)
    own_segment = (lane_segment == lax.broadcasted_iota(jnp.int32, (SEGMENTS, BLOCK), 0)).astype(f32)

    def clear(place, steep):
        grad_ref[place] = jnp.zeros(grad_ref.shape[1:], f32)
        forms = arrived_ref[place, :, 2 * BLOCK : 5 * BLOCK]
        return jnp.maximum(steep, forms * forms)

    steep = lax.fori_loop(0, grad_ref.shape[0], clear, jnp.zeros((1, 3 * BLOCK), f32), unroll=8)
    smooth = (
        jnp.max(steep[:, 0:BLOCK] + steep[:, BLOCK : 2 * BLOCK] + steep[:, 2 * BLOCK : 3 * BLOCK])
        <= SMOOTH_TRACE
    )
    form_ref[...] = jnp.zeros_like(form_ref)
    for empty in (tint_ref, center_ref, rows_ref, glow_ref, carry_ref, behind_ref):
        empty[...] = jnp.zeros_like(empty)
    for bank in range(2):
        rows_ref[bank, 0:8, :] = moments_ref[...]

    def clear_steps(slot, _):
        alpha_ref[1, slot] = jnp.zeros(alpha_ref.shape[2:], f32)
        weight_ref[1, slot] = jnp.zeros(weight_ref.shape[2:], f32)
        return 0

    lax.fori_loop(0, SLOTS, clear_steps, 0)

    def place_of(row, slot):
        return jnp.maximum(pairs_ref[row, slot], 0)

    def prepare(row, bank, quick):
        view = place_ref[row]
        center_x = (16 * lax.rem(view, TX) + 8).astype(f32)
        center_y = (16 * lax.div(view, TX) + 8).astype(f32)
        live = jnp.zeros((SLOTS, BLOCK), f32)
        for slot in range(SLOTS):
            live = jnp.where(slot_row == slot, (pairs_ref[row, slot] >= 0).astype(f32), live)
            place = place_of(row, slot)
            for base in range(9):
                block_ref[16 * slot + base : 16 * slot + base + 1, :] = arrived_ref[
                    place, :, BLOCK * base : BLOCK * base + BLOCK
                ]

        def fetched(base):
            return block_ref[pl.ds(base, SLOTS, stride=16), :]

        across = fetched(0) - center_x
        down = fetched(1) - center_y
        center_ref[bank, 0] = across
        center_ref[bank, 1] = down
        form_xx, form_xy, form_yy = fetched(2), fetched(3), fetched(4)
        log_opacity = jnp.where(live > 0.0, fetched(5), -1e9)
        shift_one = -(form_xx * across + form_xy * down)
        shift_two = -(form_yy * down)
        if quick:
            shift_one = jnp.clip(shift_one, -1e4, 1e4)
            shift_two = jnp.clip(shift_two, -1e4, 1e4)
            values = (
                log_opacity - shift_one * shift_one - shift_two * shift_two,
                -2.0 * (form_xx * shift_one),
                -2.0 * (form_xy * shift_one + form_yy * shift_two),
                -(form_xx * form_xx),
                -2.0 * (form_xx * form_xy),
                -(form_xy * form_xy + form_yy * form_yy),
            )
        else:
            values = (form_xx, form_xy, shift_one, form_yy, shift_two, log_opacity)
        for base, value in enumerate(values):
            for part, piece in enumerate(split3(value)):
                form_ref[pl.ds(8 * (3 * base + part), SLOTS), :] = piece
        for channel in range(3):
            high, low = split2(fetched(6 + channel))
            for base, piece in enumerate((high, low, high)):
                tint_ref[bank, pl.ds(8 * (3 * base + channel), SLOTS), :] = piece

    def exponents(slot, bank, quick):
        lhs = form_ref[pl.ds(slot, 32, stride=8), :].astype(bf16)
        if quick:
            power_ref[bank, slot] = lax.dot_general(
                lhs, quadratic_ref[...], CONTRACT_ROWS, preferred_element_type=f32
            )
            return
        steep_ref[...] = lax.dot_general(lhs, forms_ref[...], CONTRACT_ROWS, preferred_element_type=f32)

    def joined(kept, inner):
        halves = [jnp.concatenate([piece for part in kept[2 * inner + half] for piece in part], axis=0) for half in range(2)]
        return jnp.concatenate(halves, axis=1)

    def ahead(slots, bank, quick):
        chains = [(inner, half) for inner in range(len(slots)) for half in range(2)]
        trans = [jnp.ones((SEGMENTS, 128), f32) for _ in chains]
        kept = [[[None] * (STEPS // 2) for _ in range(2)] for _ in chains]

        def keep(chain, pair, value):
            high = value.astype(bf16)
            kept[chain][0][pair] = high
            kept[chain][1][pair] = (value - high.astype(f32)).astype(bf16)

        for pair in range(STEPS // 2):
            weights = [[] for _ in chains]
            for step in (2 * pair, 2 * pair + 1):
                eight = slice(8 * step, 8 * step + 8)
                for chain, (inner, half) in enumerate(chains):
                    lanes = slice(128 * half, 128 * half + 128)
                    if quick:
                        exponent = jnp.minimum(power_ref[bank, slots[inner], eight, lanes], 0.0)
                    else:
                        one = steep_ref[eight, lanes]
                        two = steep_ref[eight, 256 + 128 * half : 384 + 128 * half]
                        three = steep_ref[eight, 512 + 128 * half : 640 + 128 * half]
                        exponent = three - one * one - two * two
                    alpha = jnp.exp2(exponent)
                    weight = alpha * trans[chain]
                    trans[chain] = trans[chain] - weight
                    alpha_ref[bank, slots[inner], eight, lanes] = alpha
                    weight_ref[bank, slots[inner], eight, lanes] = weight
                    weights[chain].append(weight)
            for chain in range(len(chains)):
                keep(chain, pair, jnp.concatenate(weights[chain], axis=0))
        for chain, (inner, half) in enumerate(chains):
            trans_ref[slots[inner], :, 128 * half : 128 * half + 128] = trans[chain]
        for inner, slot in enumerate(slots):
            parts = [own_segment * tint_ref[bank, pl.ds(8 * base + slot, 1), :] for base in range(6)]
            lhs = jnp.concatenate(parts, axis=0).astype(bf16)
            found = lax.dot_general(
                jnp.concatenate([lhs, lhs], axis=1), joined(kept, inner),
                (((1,), (0,)), ((), ())), preferred_element_type=f32,
            )
            local_ref[slot] = found[0:24] + found[24:48]

    def middle(row, bank):
        before = jnp.ones((1, PIXELS), f32)
        seen = [jnp.zeros((SEGMENTS, PIXELS), f32) for _ in range(3)]
        for slot in range(SLOTS):
            through = trans_ref[slot]
            for reach in (1, 2, 4):
                through = through * jnp.where(segment >= reach, pltpu.roll(through, reach, 0), 1.0)
            carry = jnp.where(segment >= 1, pltpu.roll(through, 1, 0), 1.0) * before
            carry_ref[bank, slot] = carry
            for channel in range(3):
                seen[channel] = seen[channel] + carry * local_ref[slot, 8 * channel : 8 * channel + 8, :]
            before = before * through[7:8]
        glow = []
        for channel in range(3):
            color = jnp.sum(seen[channel], axis=0, keepdims=True)
            image_ref[channel, pl.ds(row, 1), :] = color
            value = (color - target_ref[channel, pl.ds(row, 1), :]) * (2.0 / 512.0)
            glow.append(value)
            high, low = split2(value)
            for base, piece in enumerate((high, high, low)):
                glow_ref[bank, 3 * base + channel : 3 * base + channel + 1, :] = piece
            rows_ref[bank, 8 + channel : 9 + channel, :] = high
            rows_ref[bank, 16 + channel : 17 + channel, :] = low

        after = jnp.zeros((1, PIXELS), f32)
        for slot in reversed(range(SLOTS)):
            through = trans_ref[slot]
            light = (
                local_ref[slot, 0:8, :] * glow[0]
                + local_ref[slot, 8:16, :] * glow[1]
                + local_ref[slot, 16:24, :] * glow[2]
            )
            for reach in (1, 2, 4):
                inside = segment < SEGMENTS - reach
                light = light + through * jnp.where(inside, pltpu.roll(light, SEGMENTS - reach, 0), 0.0)
                through = through * jnp.where(inside, pltpu.roll(through, SEGMENTS - reach, 0), 1.0)
            start = light + through * after
            behind_ref[bank, slot] = jnp.where(segment < SEGMENTS - 1, pltpu.roll(start, SEGMENTS - 1, 0), after)
            after = start[0:1]

    def glows(slot, bank):
        glow_power_ref[bank, slot] = lax.dot_general(
            tint_ref[bank, pl.ds(slot, 16, stride=8), :].astype(bf16), glow_ref[bank].astype(bf16),
            CONTRACT_ROWS, preferred_element_type=f32,
        )

    def back(slots, bank):
        chains = [(inner, half) for inner in range(len(slots)) for half in range(2)]
        behind = [behind_ref[bank, slots[inner], :, 128 * half : 128 * half + 128] for inner, half in chains]
        kept = [[[None] * (STEPS // 2) for _ in range(4)] for _ in chains]
        for pair in reversed(range(STEPS // 2)):
            pulls = [[] for _ in chains]
            weights = [[] for _ in chains]
            for step in (2 * pair + 1, 2 * pair):
                eight = slice(8 * step, 8 * step + 8)
                for chain, (inner, half) in enumerate(chains):
                    lanes = slice(128 * half, 128 * half + 128)
                    alpha = alpha_ref[bank, slots[inner], eight, lanes]
                    carry = carry_ref[bank, slots[inner], :, lanes]
                    weight = weight_ref[bank, slots[inner], eight, lanes] * carry
                    gain = glow_power_ref[bank, slots[inner], eight, lanes] - behind[chain]
                    behind[chain] = behind[chain] + alpha * gain
                    pulls[chain].append(weight * gain)
                    weights[chain].append(weight)
            for chain in range(len(chains)):
                for base, parts in ((0, pulls[chain]), (2, weights[chain])):
                    value = jnp.concatenate([parts[1], parts[0]], axis=0)
                    high = value.astype(bf16)
                    kept[chain][base][pair] = high
                    kept[chain][base + 1][pair] = (value - high.astype(f32)).astype(bf16)
        lhs_rows = rows_ref[bank].astype(bf16)
        for inner, slot in enumerate(slots):
            found = lax.dot_general(
                lhs_rows, joined(kept, inner), CONTRACT_LANES, preferred_element_type=f32
            )
            tints = found[8:24, 256:384] + found[8:24, 384:512]
            sums_ref[pl.ds(16 * slot, 8), :] = found[0:8, 0:128] + found[0:8, 128:256]
            sums_ref[pl.ds(16 * slot + 8, 8), :] = tints[0:8] + tints[8:16]

    def finish(row, bank):
        across = center_ref[bank, 0]
        down = center_ref[bank, 1]

        def summed(base):
            return sums_ref[pl.ds(base, SLOTS, stride=16), :]

        total, sum_x, sum_y = summed(0), summed(1), summed(2)
        off_x = sum_x - across * total
        off_y = sum_y - down * total
        sum_xx = summed(3) - across * (sum_x + off_x)
        sum_xy = summed(4) - across * sum_y - down * off_x
        sum_yy = summed(5) - down * (sum_y + off_y)
        values = (off_x, off_y, sum_xx, sum_xy, sum_yy, total, summed(8), summed(9), summed(10))
        for base, value in enumerate(values):
            sums_ref[pl.ds(base, SLOTS, stride=16), :] = value
        for slot in range(SLOTS):
            place = place_of(row, slot)
            for base in range(9):
                lanes = slice(BLOCK * base, BLOCK * base + BLOCK)
                grad_ref[place, :, lanes] = (
                    grad_ref[place, :, lanes] + sums_ref[16 * slot + base : 16 * slot + base + 1, :]
                )

    groups = [list(range(first, first + GROUP)) for first in range(0, SLOTS, GROUP)]

    def both(row, bank):
        prepare(row, bank, True)
        for slot in range(SLOTS):
            exponents(slot, bank, True)
            glows(slot, 1 - bank)
        for group in groups:
            ahead(group, bank, True)
            back(group, 1 - bank)
        finish(jnp.maximum(row - 1, 0), 1 - bank)
        middle(row, bank)

    @pl.when(smooth)
    def _():
        def two(pair, _):
            both(2 * pair, 0)
            both(2 * pair + 1, 1)
            return 0

        lax.fori_loop(0, tiles // 2, two, 0)
        for slot in range(SLOTS):
            glows(slot, 1)
        for group in groups:
            back(group, 1)
        finish(tiles - 1, 1)

    @pl.when(jnp.logical_not(smooth))
    def _():
        def tile(row, _):
            def forth(slot, _):
                exponents(slot, 0, False)
                ahead([slot], 0, False)
                return 0

            def back_one(slot, _):
                glows(slot, 0)
                back([slot], 0)
                return 0

            prepare(row, 0, False)
            lax.fori_loop(0, SLOTS, forth, 0)
            middle(row, 0)
            lax.fori_loop(0, SLOTS, back_one, 0)
            finish(row, 0)
            return 0

        lax.fori_loop(0, tiles, tile, 0)


def blend(pairs, tile_place, arrived, target):
    quadratic, forms, moments = pixel_tables()
    tiles = target.shape[1]
    f32 = jnp.float32
    bf16 = jnp.bfloat16
    vmem = pl.BlockSpec(memory_space=pltpu.VMEM)
    smem = pl.BlockSpec(memory_space=pltpu.SMEM)
    return pl.pallas_call(
        blend_kernel,
        out_shape=(
            jax.ShapeDtypeStruct((3, tiles, PIXELS), f32),
            jax.ShapeDtypeStruct(arrived.shape, f32),
        ),
        in_specs=[smem, smem, vmem, vmem, vmem, vmem, vmem],
        out_specs=(vmem, vmem),
        scratch_shapes=[
            pltpu.VMEM((SLOTS * 16, BLOCK), f32),
            pltpu.VMEM((32 * SLOTS, BLOCK), f32),
            pltpu.VMEM((2, 16 * SLOTS, BLOCK), f32),
            pltpu.VMEM((2, 2, SLOTS, BLOCK), f32),
            pltpu.VMEM((BLOCK, 3 * PIXELS), f32),
            pltpu.VMEM((2, SLOTS, BLOCK, PIXELS), f32),
            pltpu.VMEM((2, SLOTS, BLOCK, PIXELS), f32),
            pltpu.VMEM((2, SLOTS, BLOCK, PIXELS), f32),
            pltpu.VMEM((2, SLOTS, BLOCK, PIXELS), f32),
            pltpu.VMEM((SLOTS, SEGMENTS, PIXELS), f32),
            pltpu.VMEM((SLOTS, 3 * SEGMENTS, PIXELS), f32),
            pltpu.VMEM((2, SLOTS, SEGMENTS, PIXELS), f32),
            pltpu.VMEM((2, SLOTS, SEGMENTS, PIXELS), f32),
            pltpu.VMEM((2, 16, PIXELS), f32),
            pltpu.VMEM((2, 32, PIXELS), f32),
            pltpu.VMEM((SLOTS * 16, BLOCK), f32),
        ],
        compiler_params=pltpu.CompilerParams(vmem_limit_bytes=48 << 20),
        cost_estimate=pl.CostEstimate(flops=200_000_000, bytes_accessed=6_000_000, transcendentals=4_000_000),
        name="blend",
    )(
        pairs, tile_place, arrived, target, jnp.asarray(quadratic, bf16),
        jnp.asarray(forms, bf16), jnp.asarray(moments, f32),
    )


def screen_of(raw, width, height):
    place_x, place_y, place_z = raw[0], raw[1], raw[2]
    screen_u = width * place_x / place_z + 0.5 * width
    screen_v = width * place_y / place_z + 0.5 * height
    inverse_one = jnp.exp(-2.0 * raw[3])
    inverse_two = jnp.exp(-2.0 * raw[4])
    cosine = jnp.cos(raw[5])
    sine = jnp.sin(raw[5])
    conic_a = cosine * cosine * inverse_one + sine * sine * inverse_two
    conic_b = cosine * sine * (inverse_one - inverse_two)
    conic_c = sine * sine * inverse_one + cosine * cosine * inverse_two
    log_opacity = jnp.minimum(raw[6], 0.0) - jnp.log1p(jnp.exp(-jnp.abs(raw[6])))
    length = jnp.sqrt(place_x * place_x + place_y * place_y + place_z * place_z)
    basis = harmonics(place_x / length, place_y / length, place_z / length)
    colors = []
    for channel in range(3):
        color = raw[7 + 16 * channel] * basis[0]
        for term in range(1, 16):
            color = color + raw[7 + 16 * channel + term] * basis[term]
        colors.append(0.5 + color)
    return [screen_u, screen_v, conic_a, conic_b, conic_c, log_opacity] + colors


def permuted(value, order):
    high, middle, low = (part.astype(jnp.bfloat16) for part in split3(value))
    rows = value.shape[0]
    found = jnp.dot(jnp.concatenate([high, middle, low], axis=0), order, preferred_element_type=jnp.float32)
    return found[0:rows] + found[rows : 2 * rows] + found[2 * rows : 3 * rows]


def project_kernel(width, height, splats_ref, order_ref, rows_ref):
    params, blocks, _ = splats_ref.shape
    raw = [splats_ref[base] for base in range(params)]
    found = screen_of(raw, width, height)
    conic_a, conic_b, conic_c = found[2:5]
    steep = conic_a > 1e-30
    over = lax.rsqrt(jnp.where(steep, conic_a, 1.0))
    form_xx = jnp.sqrt(conic_a)
    form_xy = jnp.where(steep, conic_b * over, 0.0)
    form_yy = jnp.where(steep, jnp.exp(-raw[3] - raw[4]) * over, jnp.sqrt(conic_c))
    rows = [found[0], found[1], FORM_SCALE * form_xx, FORM_SCALE * form_xy, FORM_SCALE * form_yy, LOG2_E * found[5]]
    for base, value in enumerate(rows + found[6:9]):
        value = permuted(value, order_ref[...])
        for block in range(blocks):
            rows_ref[block, :, BLOCK * base : BLOCK * base + BLOCK] = value[block : block + 1, :]


def project(splats, width, height):
    _, blocks, lanes = splats.shape
    vmem = pl.BlockSpec(memory_space=pltpu.VMEM)
    return pl.pallas_call(
        functools.partial(project_kernel, width, height),
        out_shape=jax.ShapeDtypeStruct((blocks, 1, 9 * lanes), jnp.float32),
        in_specs=[vmem, vmem],
        out_specs=vmem,
        cost_estimate=pl.CostEstimate(flops=5_000_000, bytes_accessed=1_000_000, transcendentals=30_000),
        name="project",
    )(splats, jnp.asarray(lane_order(), jnp.bfloat16))


def pack_kernel(asked_ref, rows_ref, payload_ref):
    def one(owner, _):
        for which in range(asked_ref.shape[2]):
            place = owner * asked_ref.shape[2] + which
            payload_ref[place] = rows_ref[jnp.maximum(asked_ref[owner, 0, which], 0)]
        return 0

    lax.fori_loop(0, asked_ref.shape[0], one, 0, unroll=8)


def pack(asked, rows):
    vmem = pl.BlockSpec(memory_space=pltpu.VMEM)
    return pl.pallas_call(
        pack_kernel,
        out_shape=jax.ShapeDtypeStruct((asked.shape[0] * asked.shape[2],) + rows.shape[1:], jnp.float32),
        in_specs=[pl.BlockSpec(memory_space=pltpu.SMEM), vmem],
        out_specs=vmem,
        cost_estimate=pl.CostEstimate(flops=0, bytes_accessed=2_000_000, transcendentals=0),
        name="pack",
    )(asked, rows)


def update_kernel(
    width, height, asked_ref, returned_ref, splats_ref, one_ref, two_ref, order_ref,
    grad_ref, step_ref, sum_ref, rows_ref, pulled_ref, *lane_refs,
):
    params, blocks, _ = splats_ref.shape
    for lane_ref in lane_refs:
        lane_ref[...] = jnp.zeros_like(lane_ref)

    def gather(group, _):
        for lane, lane_ref in enumerate(lane_refs):
            place = group * len(lane_refs) + lane
            which = lax.rem(place, asked_ref.shape[2])
            block = jnp.maximum(asked_ref[lax.div(place, asked_ref.shape[2]), 0, which], 0)
            lane_ref[block] = lane_ref[block] + returned_ref[place]
        return 0

    lax.fori_loop(0, returned_ref.shape[0] // len(lane_refs), gather, 0, unroll=2)
    for block in range(blocks):
        value = lane_refs[0][block]
        for lane_ref in lane_refs[1:]:
            value = value + lane_ref[block]
        sum_ref[block] = value
        for base in range(9):
            rows_ref[blocks * base + block : blocks * base + block + 1, :] = sum_ref[
                block, :, BLOCK * base : BLOCK * base + BLOCK
            ]
    pulled_ref[...] = permuted(rows_ref[...], order_ref[...])
    for first in range(0, blocks, 8):
        eight = slice(first, first + 8)
        raw = [splats_ref[base, eight, :] for base in range(params)]
        summed = [pulled_ref[blocks * base + first : blocks * base + first + 8, :] for base in range(9)]
        found, pull = jax.vjp(functools.partial(screen_of, width=width, height=height), raw)
        conic_a, conic_b, conic_c = found[2:5]
        (pulled,) = pull(
            [
                conic_a * summed[0] + conic_b * summed[1],
                conic_b * summed[0] + conic_c * summed[1],
                -0.5 * summed[2],
                -summed[3],
                -0.5 * summed[4],
                summed[5],
            ]
            + summed[6:9]
        )
        for base, grad in enumerate(pulled):
            grad_ref[base, eight, :] = grad
            moved = 0.9 * one_ref[base, eight, :] + 0.1 * grad
            second = 0.999 * two_ref[base, eight, :] + 0.001 * grad * grad
            step_ref[base, eight, :] = moved / (jnp.sqrt(second) + 1e-08)


def update(asked, returned, splats, moment_one, moment_two, width, height):
    params, blocks, lanes = splats.shape
    vmem = pl.BlockSpec(memory_space=pltpu.VMEM)
    f32 = jnp.float32
    shape = jax.ShapeDtypeStruct(splats.shape, f32)
    row_sums = pltpu.VMEM((blocks, 1, 9 * lanes), f32)
    return pl.pallas_call(
        functools.partial(update_kernel, width, height),
        out_shape=(shape, shape),
        in_specs=[pl.BlockSpec(memory_space=pltpu.SMEM)] + [vmem] * 5,
        out_specs=(vmem, vmem),
        scratch_shapes=[
            row_sums,
            pltpu.VMEM((9 * blocks, lanes), f32),
            pltpu.VMEM((9 * blocks, lanes), f32),
        ]
        + [row_sums] * 4,
        cost_estimate=pl.CostEstimate(flops=8_000_000, bytes_accessed=6_000_000, transcendentals=500_000),
        name="update",
    )(asked, returned, splats, moment_one, moment_two, jnp.asarray(lane_order().T, jnp.bfloat16))


def trade(payload):
    return lax.all_to_all(payload, ("gx", "gy"), split_axis=0, concat_axis=0, tiled=True)


def local(splats, moment_one, moment_two, target, tile_place, pairs, fetch):
    devices = lax.axis_size("gx") * lax.axis_size("gy")
    tiles_here = target.shape[0]
    width = 16.0 * TX
    height = 16.0 * (tiles_here * devices // TX)
    flat, first_moment, second_moment = (
        jnp.transpose(value, (1, 0, 2)) for value in (splats, moment_one, moment_two)
    )
    asked = trade(fetch.reshape(fetch.shape[1], 1, fetch.shape[2]))
    rows = project(flat, width, height)
    arrived = trade(pack(asked, rows))
    image, received = blend(pairs, tile_place, arrived, jnp.transpose(target, (1, 0, 2)))
    grad, step = update(asked, trade(received), flat, first_moment, second_moment, width, height)
    return tuple(jnp.transpose(value, (1, 0, 2)) for value in (image, grad, step))


def solution(mesh):
    return jax.shard_map(
        local,
        mesh=mesh,
        in_specs=(
            P(("gx", "gy"), None, None),
            P(("gx", "gy"), None, None),
            P(("gx", "gy"), None, None),
            P(("gx", "gy"), None, None),
            P(("gx", "gy")),
            P(("gx", "gy"), None),
            P(("gx", "gy"), None, None),
        ),
        out_specs=(
            P(("gx", "gy"), None, None),
            P(("gx", "gy"), None, None),
            P(("gx", "gy"), None, None),
        ),
        check_vma=False,
    )
```

```python
import functools

import jax
import jax.numpy as jnp
import numpy as np
from jax import lax
from jax.experimental import pallas as pl
from jax.experimental.pallas import tpu as pltpu
from jax.sharding import PartitionSpec as P

TX = 16
BLOCK = 128
SEGMENTS = 8
STEPS = BLOCK // SEGMENTS
SLOTS = 8
PIXELS = 256
LOG2_E = 1.4426950408889634
FORM_SCALE = 0.8493218002880191
SMOOTH_TRACE = 0.75
GROUP = 2
PARTS = 4

HARMONIC_ZERO = 0.28209479177387814
HARMONIC_ONE = 0.4886025119029199
HARMONIC_TWO = (
    1.0925484305920792,
    -1.0925484305920792,
    0.31539156525252005,
    -1.0925484305920792,
    0.5462742152960396,
)
HARMONIC_THREE = (
    -0.5900435899266435,
    2.890611442640554,
    -0.4570457994644658,
    0.3731763325901154,
    -0.4570457994644658,
    1.445305721320277,
    -0.5900435899266435,
)


def harmonics(east, north, ahead):
    east_east = east * east
    north_north = north * north
    ahead_ahead = ahead * ahead
    terms = [
        jnp.full_like(east, HARMONIC_ZERO),
        -HARMONIC_ONE * north,
        HARMONIC_ONE * ahead,
        -HARMONIC_ONE * east,
        HARMONIC_TWO[0] * east * north,
        HARMONIC_TWO[1] * north * ahead,
        HARMONIC_TWO[2] * (2.0 * ahead_ahead - east_east - north_north),
        HARMONIC_TWO[3] * east * ahead,
        HARMONIC_TWO[4] * (east_east - north_north),
        HARMONIC_THREE[0] * north * (3.0 * east_east - north_north),
        HARMONIC_THREE[1] * east * north * ahead,
        HARMONIC_THREE[2] * north * (4.0 * ahead_ahead - east_east - north_north),
        HARMONIC_THREE[3] * ahead * (2.0 * ahead_ahead - 3.0 * east_east - 3.0 * north_north),
        HARMONIC_THREE[4] * east * (4.0 * ahead_ahead - east_east - north_north),
        HARMONIC_THREE[5] * ahead * (east_east - north_north),
        HARMONIC_THREE[6] * east * (east_east - 3.0 * north_north),
    ]
    return terms


def lane_order():
    order = np.zeros((BLOCK, BLOCK), np.float32)
    for step in range(STEPS):
        for segment in range(SEGMENTS):
            order[STEPS * segment + step, SEGMENTS * step + segment] = 1.0
    return order


def pixel_tables():
    pixel = np.arange(PIXELS)
    across = (pixel % 16) - 7.5
    down = (pixel // 16) - 7.5
    ones = np.ones(PIXELS)
    moments = np.zeros((8, PIXELS), np.float32)
    moments[0:6] = [ones, across, down, across * across, across * down, down * down]
    quadratic = np.zeros((32, PIXELS), np.float32)
    for base in range(6):
        quadratic[3 * base : 3 * base + 3] = moments[base]
    forms = np.zeros((32, 3 * PIXELS), np.float32)
    forms[0:3, :PIXELS] = across
    forms[3:6, :PIXELS] = down
    forms[6:9, :PIXELS] = ones
    forms[9:12, PIXELS : 2 * PIXELS] = down
    forms[12:15, PIXELS : 2 * PIXELS] = ones
    forms[15:18, 2 * PIXELS :] = ones
    return quadratic, forms, moments


def rounded(value):
    return value.astype(jnp.bfloat16).astype(jnp.float32)


def split3(value):
    high = rounded(value)
    rest = value - high
    middle = rounded(rest)
    return high, middle, rest - middle


def split2(value):
    high = rounded(value)
    return high, rounded(value - high)


CONTRACT_ROWS = (((0,), (0,)), ((), ()))
CONTRACT_LANES = (((1,), (1,)), ((), ()))


def blend_kernel(
    pairs_ref, place_ref, arrived_ref, target_ref, quadratic_ref, forms_ref, moments_ref,
    image_ref, grad_ref,
    block_ref, form_ref, tint_ref, center_ref, steep_ref, power_ref, glow_power_ref,
    alpha_ref, weight_ref, trans_ref, local_ref, carry_ref, behind_ref, glow_ref, rows_ref,
    sums_ref,
):
    f32 = jnp.float32
    bf16 = jnp.bfloat16
    tiles = target_ref.shape[1]
    segment = lax.broadcasted_iota(jnp.int32, (SEGMENTS, PIXELS), 0)
    slot_row = lax.broadcasted_iota(jnp.int32, (SLOTS, BLOCK), 0)
    lane_segment = lax.rem(lax.broadcasted_iota(jnp.int32, (SEGMENTS, BLOCK), 1), SEGMENTS)
    own_segment = (lane_segment == lax.broadcasted_iota(jnp.int32, (SEGMENTS, BLOCK), 0)).astype(f32)

    def clear(place, steep):
        grad_ref[place] = jnp.zeros(grad_ref.shape[1:], f32)
        forms = arrived_ref[place, :, 2 * BLOCK : 5 * BLOCK]
        return jnp.maximum(steep, forms * forms)

    steep = lax.fori_loop(0, grad_ref.shape[0], clear, jnp.zeros((1, 3 * BLOCK), f32), unroll=8)
    smooth = (
        jnp.max(steep[:, 0:BLOCK] + steep[:, BLOCK : 2 * BLOCK] + steep[:, 2 * BLOCK : 3 * BLOCK])
        <= SMOOTH_TRACE
    )
    form_ref[...] = jnp.zeros_like(form_ref)
    for empty in (tint_ref, center_ref, rows_ref, glow_ref, carry_ref, behind_ref):
        empty[...] = jnp.zeros_like(empty)
    for bank in range(2):
        rows_ref[bank, 0:8, :] = moments_ref[...]

    def clear_steps(slot, _):
        alpha_ref[1, slot] = jnp.zeros(alpha_ref.shape[2:], f32)
        weight_ref[1, slot] = jnp.zeros(weight_ref.shape[2:], f32)
        return 0

    lax.fori_loop(0, SLOTS, clear_steps, 0)

    def place_of(row, slot):
        return jnp.maximum(pairs_ref[row, slot], 0)

    def prepare(row, bank, quick):
        view = place_ref[row]
        center_x = (16 * lax.rem(view, TX) + 8).astype(f32)
        center_y = (16 * lax.div(view, TX) + 8).astype(f32)
        live = jnp.zeros((SLOTS, BLOCK), f32)
        for slot in range(SLOTS):
            live = jnp.where(slot_row == slot, (pairs_ref[row, slot] >= 0).astype(f32), live)
            place = place_of(row, slot)
            for base in range(9):
                block_ref[16 * slot + base : 16 * slot + base + 1, :] = arrived_ref[
                    place, :, BLOCK * base : BLOCK * base + BLOCK
                ]

        def fetched(base):
            return block_ref[pl.ds(base, SLOTS, stride=16), :]

        across = fetched(0) - center_x
        down = fetched(1) - center_y
        center_ref[bank, 0] = across
        center_ref[bank, 1] = down
        form_xx, form_xy, form_yy = fetched(2), fetched(3), fetched(4)
        log_opacity = jnp.where(live > 0.0, fetched(5), -1e9)
        shift_one = -(form_xx * across + form_xy * down)
        shift_two = -(form_yy * down)
        if quick:
            shift_one = jnp.clip(shift_one, -1e4, 1e4)
            shift_two = jnp.clip(shift_two, -1e4, 1e4)
            values = (
                log_opacity - shift_one * shift_one - shift_two * shift_two,
                -2.0 * (form_xx * shift_one),
                -2.0 * (form_xy * shift_one + form_yy * shift_two),
                -(form_xx * form_xx),
                -2.0 * (form_xx * form_xy),
                -(form_xy * form_xy + form_yy * form_yy),
            )
        else:
            values = (form_xx, form_xy, shift_one, form_yy, shift_two, log_opacity)
        for base, value in enumerate(values):
            for part, piece in enumerate(split3(value)):
                form_ref[pl.ds(8 * (3 * base + part), SLOTS), :] = piece
        for channel in range(3):
            high, low = split2(fetched(6 + channel))
            for base, piece in enumerate((high, low, high)):
                tint_ref[bank, pl.ds(8 * (3 * base + channel), SLOTS), :] = piece

    def exponents(slot, bank, quick):
        lhs = form_ref[pl.ds(slot, 32, stride=8), :].astype(bf16)
        if quick:
            power_ref[bank, slot] = lax.dot_general(
                lhs, quadratic_ref[...], CONTRACT_ROWS, preferred_element_type=f32
            )
            return
        steep_ref[...] = lax.dot_general(lhs, forms_ref[...], CONTRACT_ROWS, preferred_element_type=f32)

    def joined(kept, inner):
        halves = [jnp.concatenate([piece for part in kept[2 * inner + half] for piece in part], axis=0) for half in range(2)]
        return jnp.concatenate(halves, axis=1)

    def ahead(slots, bank, quick):
        chains = [(inner, half) for inner in range(len(slots)) for half in range(2)]
        trans = [jnp.ones((SEGMENTS, 128), f32) for _ in chains]
        kept = [[[None] * (STEPS // 2) for _ in range(2)] for _ in chains]

        def keep(chain, pair, value):
            high = value.astype(bf16)
            kept[chain][0][pair] = high
            kept[chain][1][pair] = (value - high.astype(f32)).astype(bf16)

        for pair in range(STEPS // 2):
            weights = [[] for _ in chains]
            for step in (2 * pair, 2 * pair + 1):
                eight = slice(8 * step, 8 * step + 8)
                for chain, (inner, half) in enumerate(chains):
                    lanes = slice(128 * half, 128 * half + 128)
                    if quick:
                        exponent = jnp.minimum(power_ref[bank, slots[inner], eight, lanes], 0.0)
                    else:
                        one = steep_ref[eight, lanes]
                        two = steep_ref[eight, 256 + 128 * half : 384 + 128 * half]
                        three = steep_ref[eight, 512 + 128 * half : 640 + 128 * half]
                        exponent = three - one * one - two * two
                    alpha = jnp.exp2(exponent)
                    weight = alpha * trans[chain]
                    trans[chain] = trans[chain] - weight
                    alpha_ref[bank, slots[inner], eight, lanes] = alpha
                    weight_ref[bank, slots[inner], eight, lanes] = weight
                    weights[chain].append(weight)
            for chain in range(len(chains)):
                keep(chain, pair, jnp.concatenate(weights[chain], axis=0))
        for chain, (inner, half) in enumerate(chains):
            trans_ref[slots[inner], :, 128 * half : 128 * half + 128] = trans[chain]
        for inner, slot in enumerate(slots):
            parts = [own_segment * tint_ref[bank, pl.ds(8 * base + slot, 1), :] for base in range(6)]
            lhs = jnp.concatenate(parts, axis=0).astype(bf16)
            found = lax.dot_general(
                jnp.concatenate([lhs, lhs], axis=1), joined(kept, inner),
                (((1,), (0,)), ((), ())), preferred_element_type=f32,
            )
            local_ref[slot] = found[0:24] + found[24:48]

    def middle(row, bank):
        before = jnp.ones((1, PIXELS), f32)
        seen = [jnp.zeros((SEGMENTS, PIXELS), f32) for _ in range(3)]
        for slot in range(SLOTS):
            through = trans_ref[slot]
            for reach in (1, 2, 4):
                through = through * jnp.where(segment >= reach, pltpu.roll(through, reach, 0), 1.0)
            carry = jnp.where(segment >= 1, pltpu.roll(through, 1, 0), 1.0) * before
            carry_ref[bank, slot] = carry
            for channel in range(3):
                seen[channel] = seen[channel] + carry * local_ref[slot, 8 * channel : 8 * channel + 8, :]
            before = before * through[7:8]
        glow = []
        for channel in range(3):
            color = jnp.sum(seen[channel], axis=0, keepdims=True)
            image_ref[channel, pl.ds(row, 1), :] = color
            value = (color - target_ref[channel, pl.ds(row, 1), :]) * (2.0 / 512.0)
            glow.append(value)
            high, low = split2(value)
            for base, piece in enumerate((high, high, low)):
                glow_ref[bank, 3 * base + channel : 3 * base + channel + 1, :] = piece
            rows_ref[bank, 8 + channel : 9 + channel, :] = high
            rows_ref[bank, 16 + channel : 17 + channel, :] = low

        after = jnp.zeros((1, PIXELS), f32)
        for slot in reversed(range(SLOTS)):
            through = trans_ref[slot]
            light = (
                local_ref[slot, 0:8, :] * glow[0]
                + local_ref[slot, 8:16, :] * glow[1]
                + local_ref[slot, 16:24, :] * glow[2]
            )
            for reach in (1, 2, 4):
                inside = segment < SEGMENTS - reach
                light = light + through * jnp.where(inside, pltpu.roll(light, SEGMENTS - reach, 0), 0.0)
                through = through * jnp.where(inside, pltpu.roll(through, SEGMENTS - reach, 0), 1.0)
            start = light + through * after
            behind_ref[bank, slot] = jnp.where(segment < SEGMENTS - 1, pltpu.roll(start, SEGMENTS - 1, 0), after)
            after = start[0:1]

    def glows(slot, bank):
        glow_power_ref[bank, slot] = lax.dot_general(
            tint_ref[bank, pl.ds(slot, 16, stride=8), :].astype(bf16), glow_ref[bank].astype(bf16),
            CONTRACT_ROWS, preferred_element_type=f32,
        )

    def back(slots, bank):
        chains = [(inner, half) for inner in range(len(slots)) for half in range(2)]
        behind = [behind_ref[bank, slots[inner], :, 128 * half : 128 * half + 128] for inner, half in chains]
        kept = [[[None] * (STEPS // 2) for _ in range(4)] for _ in chains]
        for pair in reversed(range(STEPS // 2)):
            pulls = [[] for _ in chains]
            weights = [[] for _ in chains]
            for step in (2 * pair + 1, 2 * pair):
                eight = slice(8 * step, 8 * step + 8)
                for chain, (inner, half) in enumerate(chains):
                    lanes = slice(128 * half, 128 * half + 128)
                    alpha = alpha_ref[bank, slots[inner], eight, lanes]
                    carry = carry_ref[bank, slots[inner], :, lanes]
                    weight = weight_ref[bank, slots[inner], eight, lanes] * carry
                    gain = glow_power_ref[bank, slots[inner], eight, lanes] - behind[chain]
                    behind[chain] = behind[chain] + alpha * gain
                    pulls[chain].append(weight * gain)
                    weights[chain].append(weight)
            for chain in range(len(chains)):
                for base, parts in ((0, pulls[chain]), (2, weights[chain])):
                    value = jnp.concatenate([parts[1], parts[0]], axis=0)
                    high = value.astype(bf16)
                    kept[chain][base][pair] = high
                    kept[chain][base + 1][pair] = (value - high.astype(f32)).astype(bf16)
        lhs_rows = rows_ref[bank].astype(bf16)
        for inner, slot in enumerate(slots):
            found = lax.dot_general(
                lhs_rows, joined(kept, inner), CONTRACT_LANES, preferred_element_type=f32
            )
            tints = found[8:24, 256:384] + found[8:24, 384:512]
            sums_ref[pl.ds(16 * slot, 8), :] = found[0:8, 0:128] + found[0:8, 128:256]
            sums_ref[pl.ds(16 * slot + 8, 8), :] = tints[0:8] + tints[8:16]

    def finish(row, bank):
        across = center_ref[bank, 0]
        down = center_ref[bank, 1]

        def summed(base):
            return sums_ref[pl.ds(base, SLOTS, stride=16), :]

        total, sum_x, sum_y = summed(0), summed(1), summed(2)
        off_x = sum_x - across * total
        off_y = sum_y - down * total
        sum_xx = summed(3) - across * (sum_x + off_x)
        sum_xy = summed(4) - across * sum_y - down * off_x
        sum_yy = summed(5) - down * (sum_y + off_y)
        values = (off_x, off_y, sum_xx, sum_xy, sum_yy, total, summed(8), summed(9), summed(10))
        for base, value in enumerate(values):
            sums_ref[pl.ds(base, SLOTS, stride=16), :] = value
        for slot in range(SLOTS):
            place = place_of(row, slot)
            for base in range(9):
                lanes = slice(BLOCK * base, BLOCK * base + BLOCK)
                grad_ref[place, :, lanes] = (
                    grad_ref[place, :, lanes] + sums_ref[16 * slot + base : 16 * slot + base + 1, :]
                )

    groups = [list(range(first, first + GROUP)) for first in range(0, SLOTS, GROUP)]

    def both(row, bank):
        prepare(row, bank, True)
        for slot in range(SLOTS):
            exponents(slot, bank, True)
            glows(slot, 1 - bank)
        for group in groups:
            ahead(group, bank, True)
            back(group, 1 - bank)
        finish(jnp.maximum(row - 1, 0), 1 - bank)
        middle(row, bank)

    @pl.when(smooth)
    def _():
        def two(pair, _):
            both(2 * pair, 0)
            both(2 * pair + 1, 1)
            return 0

        lax.fori_loop(0, tiles // 2, two, 0)
        for slot in range(SLOTS):
            glows(slot, 1)
        for group in groups:
            back(group, 1)
        finish(tiles - 1, 1)

    @pl.when(jnp.logical_not(smooth))
    def _():
        def tile(row, _):
            def forth(slot, _):
                exponents(slot, 0, False)
                ahead([slot], 0, False)
                return 0

            def back_one(slot, _):
                glows(slot, 0)
                back([slot], 0)
                return 0

            prepare(row, 0, False)
            lax.fori_loop(0, SLOTS, forth, 0)
            middle(row, 0)
            lax.fori_loop(0, SLOTS, back_one, 0)
            finish(row, 0)
            return 0

        lax.fori_loop(0, tiles, tile, 0)


def blend(pairs, tile_place, arrived, target):
    quadratic, forms, moments = pixel_tables()
    tiles = target.shape[1]
    f32 = jnp.float32
    bf16 = jnp.bfloat16
    vmem = pl.BlockSpec(memory_space=pltpu.VMEM)
    smem = pl.BlockSpec(memory_space=pltpu.SMEM)
    return pl.pallas_call(
        blend_kernel,
        out_shape=(
            jax.ShapeDtypeStruct((3, tiles, PIXELS), f32),
            jax.ShapeDtypeStruct(arrived.shape, f32),
        ),
        in_specs=[smem, smem, vmem, vmem, vmem, vmem, vmem],
        out_specs=(vmem, vmem),
        scratch_shapes=[
            pltpu.VMEM((SLOTS * 16, BLOCK), f32),
            pltpu.VMEM((32 * SLOTS, BLOCK), f32),
            pltpu.VMEM((2, 16 * SLOTS, BLOCK), f32),
            pltpu.VMEM((2, 2, SLOTS, BLOCK), f32),
            pltpu.VMEM((BLOCK, 3 * PIXELS), f32),
            pltpu.VMEM((2, SLOTS, BLOCK, PIXELS), f32),
            pltpu.VMEM((2, SLOTS, BLOCK, PIXELS), f32),
            pltpu.VMEM((2, SLOTS, BLOCK, PIXELS), f32),
            pltpu.VMEM((2, SLOTS, BLOCK, PIXELS), f32),
            pltpu.VMEM((SLOTS, SEGMENTS, PIXELS), f32),
            pltpu.VMEM((SLOTS, 3 * SEGMENTS, PIXELS), f32),
            pltpu.VMEM((2, SLOTS, SEGMENTS, PIXELS), f32),
            pltpu.VMEM((2, SLOTS, SEGMENTS, PIXELS), f32),
            pltpu.VMEM((2, 16, PIXELS), f32),
            pltpu.VMEM((2, 32, PIXELS), f32),
            pltpu.VMEM((SLOTS * 16, BLOCK), f32),
        ],
        compiler_params=pltpu.CompilerParams(vmem_limit_bytes=24 << 20),
        cost_estimate=pl.CostEstimate(flops=200_000_000, bytes_accessed=6_000_000, transcendentals=4_000_000),
        name="blend",
    )(
        pairs, tile_place, arrived, target, jnp.asarray(quadratic, bf16),
        jnp.asarray(forms, bf16), jnp.asarray(moments, f32),
    )


def screen_of(raw, width, height):
    place_x, place_y, place_z = raw[0], raw[1], raw[2]
    screen_u = width * place_x / place_z + 0.5 * width
    screen_v = width * place_y / place_z + 0.5 * height
    inverse_one = jnp.exp(-2.0 * raw[3])
    inverse_two = jnp.exp(-2.0 * raw[4])
    cosine = jnp.cos(raw[5])
    sine = jnp.sin(raw[5])
    conic_a = cosine * cosine * inverse_one + sine * sine * inverse_two
    conic_b = cosine * sine * (inverse_one - inverse_two)
    conic_c = sine * sine * inverse_one + cosine * cosine * inverse_two
    log_opacity = jnp.minimum(raw[6], 0.0) - jnp.log1p(jnp.exp(-jnp.abs(raw[6])))
    length = jnp.sqrt(place_x * place_x + place_y * place_y + place_z * place_z)
    basis = harmonics(place_x / length, place_y / length, place_z / length)
    colors = []
    for channel in range(3):
        color = raw[7 + 16 * channel] * basis[0]
        for term in range(1, 16):
            color = color + raw[7 + 16 * channel + term] * basis[term]
        colors.append(0.5 + color)
    return [screen_u, screen_v, conic_a, conic_b, conic_c, log_opacity] + colors


def permuted(value, order):
    high, middle, low = (part.astype(jnp.bfloat16) for part in split3(value))
    rows = value.shape[0]
    found = jnp.dot(jnp.concatenate([high, middle, low], axis=0), order, preferred_element_type=jnp.float32)
    return found[0:rows] + found[rows : 2 * rows] + found[2 * rows : 3 * rows]


def project_kernel(width, height, splats_ref, order_ref, rows_ref):
    params, blocks, _ = splats_ref.shape
    raw = [splats_ref[base] for base in range(params)]
    found = screen_of(raw, width, height)
    conic_a, conic_b, conic_c = found[2:5]
    steep = conic_a > 1e-30
    over = lax.rsqrt(jnp.where(steep, conic_a, 1.0))
    form_xx = jnp.sqrt(conic_a)
    form_xy = jnp.where(steep, conic_b * over, 0.0)
    form_yy = jnp.where(steep, jnp.exp(-raw[3] - raw[4]) * over, jnp.sqrt(conic_c))
    rows = [found[0], found[1], FORM_SCALE * form_xx, FORM_SCALE * form_xy, FORM_SCALE * form_yy, LOG2_E * found[5]]
    for base, value in enumerate(rows + found[6:9]):
        value = permuted(value, order_ref[...])
        for block in range(blocks):
            rows_ref[block, :, BLOCK * base : BLOCK * base + BLOCK] = value[block : block + 1, :]


def project(splats, width, height):
    _, blocks, lanes = splats.shape
    vmem = pl.BlockSpec(memory_space=pltpu.VMEM)
    return pl.pallas_call(
        functools.partial(project_kernel, width, height),
        out_shape=jax.ShapeDtypeStruct((blocks, 1, 9 * lanes), jnp.float32),
        in_specs=[vmem, vmem],
        out_specs=vmem,
        cost_estimate=pl.CostEstimate(flops=5_000_000, bytes_accessed=1_000_000, transcendentals=30_000),
        compiler_params=pltpu.CompilerParams(vmem_limit_bytes=8 << 20),
        name="project",
    )(splats, jnp.asarray(lane_order(), jnp.bfloat16))


def pack_kernel(asked_ref, rows_ref, payload_ref, staged_ref, sem):
    owners, _, most = asked_ref.shape
    share = owners // PARTS
    copies = []
    for part in range(PARTS):

        def one(step, _, first=part * share):
            owner = first + step
            for which in range(most):
                staged_ref[owner * most + which] = rows_ref[jnp.maximum(asked_ref[owner, 0, which], 0)]
            return 0

        lax.fori_loop(0, share, one, 0, unroll=8)
        places = pl.ds(part * share * most, share * most)
        copies.append(pltpu.make_async_copy(staged_ref.at[places], payload_ref.at[places], sem.at[part]))
        copies[-1].start()
    for copy in copies:
        copy.wait()


def pack(asked, rows):
    vmem = pl.BlockSpec(memory_space=pltpu.VMEM)
    return pl.pallas_call(
        pack_kernel,
        out_shape=jax.ShapeDtypeStruct((asked.shape[0] * asked.shape[2],) + rows.shape[1:], jnp.float32),
        in_specs=[pl.BlockSpec(memory_space=pltpu.SMEM), vmem],
        out_specs=pl.BlockSpec(memory_space=pl.ANY),
        scratch_shapes=[
            pltpu.VMEM((asked.shape[0] * asked.shape[2],) + rows.shape[1:], jnp.float32),
            pltpu.SemaphoreType.DMA((PARTS,)),
        ],
        cost_estimate=pl.CostEstimate(flops=0, bytes_accessed=2_000_000, transcendentals=0),
        compiler_params=pltpu.CompilerParams(vmem_limit_bytes=8 << 20),
        name="pack",
    )(asked, rows)


def update_kernel(
    width, height, asked_ref, returned_ref, splats_ref, one_ref, two_ref, order_ref,
    grad_out_ref, step_out_ref, grad_ref, step_ref, sem, sum_ref, rows_ref, pulled_ref, *lane_refs,
):
    params, blocks, _ = splats_ref.shape
    for lane_ref in lane_refs:
        lane_ref[...] = jnp.zeros_like(lane_ref)

    owners, _, most = asked_ref.shape
    step = len(lane_refs) // most

    def gather(group, _):
        for lane, lane_ref in enumerate(lane_refs):
            block = jnp.maximum(asked_ref[group * step + lane // most, 0, lane % most], 0)
            lane_ref[block] = lane_ref[block] + returned_ref[group * len(lane_refs) + lane]
        return 0

    lax.fori_loop(0, owners // step, gather, 0, unroll=2)
    for block in range(blocks):
        value = lane_refs[0][block]
        for lane_ref in lane_refs[1:]:
            value = value + lane_ref[block]
        sum_ref[block] = value
        for base in range(9):
            rows_ref[blocks * base + block : blocks * base + block + 1, :] = sum_ref[
                block, :, BLOCK * base : BLOCK * base + BLOCK
            ]
    pulled_ref[...] = permuted(rows_ref[...], order_ref[...])
    copies = []
    for first in range(0, blocks, 8):
        eight = slice(first, first + 8)
        raw = [splats_ref[base, eight, :] for base in range(params)]
        summed = [pulled_ref[blocks * base + first : blocks * base + first + 8, :] for base in range(9)]
        found, pull = jax.vjp(functools.partial(screen_of, width=width, height=height), raw)
        conic_a, conic_b, conic_c = found[2:5]
        (pulled,) = pull(
            [
                conic_a * summed[0] + conic_b * summed[1],
                conic_b * summed[0] + conic_c * summed[1],
                -0.5 * summed[2],
                -summed[3],
                -0.5 * summed[4],
                summed[5],
            ]
            + summed[6:9]
        )
        for base, grad in enumerate(pulled):
            grad_ref[base, eight, :] = grad
            moved = 0.9 * one_ref[base, eight, :] + 0.1 * grad
            second = 0.999 * two_ref[base, eight, :] + 0.001 * grad * grad
            step_ref[base, eight, :] = moved / (jnp.sqrt(second) + 1e-08)
        for which, (held, out) in enumerate(((grad_ref, grad_out_ref), (step_ref, step_out_ref))):
            copies.append(
                pltpu.make_async_copy(
                    held.at[:, pl.ds(first, 8), :], out.at[:, pl.ds(first, 8), :], sem.at[first // 8, which]
                )
            )
            copies[-1].start()
    for copy in copies:
        copy.wait()


def update(asked, returned, splats, moment_one, moment_two, width, height):
    params, blocks, lanes = splats.shape
    vmem = pl.BlockSpec(memory_space=pltpu.VMEM)
    f32 = jnp.float32
    shape = jax.ShapeDtypeStruct(splats.shape, f32)
    row_sums = pltpu.VMEM((blocks, 1, 9 * lanes), f32)
    return pl.pallas_call(
        functools.partial(update_kernel, width, height),
        out_shape=(shape, shape),
        in_specs=[pl.BlockSpec(memory_space=pltpu.SMEM)] + [vmem] * 5,
        out_specs=(pl.BlockSpec(memory_space=pl.ANY), pl.BlockSpec(memory_space=pl.ANY)),
        scratch_shapes=[
            pltpu.VMEM(splats.shape, f32),
            pltpu.VMEM(splats.shape, f32),
            pltpu.SemaphoreType.DMA((blocks // 8, 2)),
            row_sums,
            pltpu.VMEM((9 * blocks, lanes), f32),
            pltpu.VMEM((9 * blocks, lanes), f32),
        ]
        + [row_sums] * 8,
        cost_estimate=pl.CostEstimate(flops=8_000_000, bytes_accessed=6_000_000, transcendentals=500_000),
        compiler_params=pltpu.CompilerParams(vmem_limit_bytes=16 << 20),
        name="update",
    )(asked, returned, splats, moment_one, moment_two, jnp.asarray(lane_order().T, jnp.bfloat16))


def trade(payload):
    return lax.all_to_all(payload, ("gx", "gy"), split_axis=0, concat_axis=0, tiled=True)


def local(splats, moment_one, moment_two, target, tile_place, pairs, fetch):
    devices = lax.axis_size("gx") * lax.axis_size("gy")
    tiles_here = target.shape[0]
    width = 16.0 * TX
    height = 16.0 * (tiles_here * devices // TX)
    flat, first_moment, second_moment = (
        jnp.transpose(value, (1, 0, 2)) for value in (splats, moment_one, moment_two)
    )
    asked = trade(fetch.reshape(fetch.shape[1], 1, fetch.shape[2]))
    rows = project(flat, width, height)
    arrived = trade(pack(asked, rows))
    image, received = blend(pairs, tile_place, arrived, jnp.transpose(target, (1, 0, 2)))
    grad, step = update(asked, trade(received), flat, first_moment, second_moment, width, height)
    return tuple(jnp.transpose(value, (1, 0, 2)) for value in (image, grad, step))


def solution(mesh):
    return jax.shard_map(
        local,
        mesh=mesh,
        in_specs=(
            P(("gx", "gy"), None, None),
            P(("gx", "gy"), None, None),
            P(("gx", "gy"), None, None),
            P(("gx", "gy"), None, None),
            P(("gx", "gy")),
            P(("gx", "gy"), None),
            P(("gx", "gy"), None, None),
        ),
        out_specs=(
            P(("gx", "gy"), None, None),
            P(("gx", "gy"), None, None),
            P(("gx", "gy"), None, None),
        ),
        check_vma=False,
    )
```

```python
import functools

import jax
import jax.numpy as jnp
import numpy as np
from jax import lax
from jax.experimental import pallas as pl
from jax.experimental.pallas import tpu as pltpu
from jax.sharding import PartitionSpec as P

TX = 16
BLOCK = 128
SEGMENTS = 8
STEPS = BLOCK // SEGMENTS
SLOTS = 8
PIXELS = 256
LOG2_E = 1.4426950408889634
FORM_SCALE = 0.8493218002880191
SMOOTH_TRACE = 0.75
GROUP = 2
PARTS = 4

HARMONIC_ZERO = 0.28209479177387814
HARMONIC_ONE = 0.4886025119029199
HARMONIC_TWO = (
    1.0925484305920792,
    -1.0925484305920792,
    0.31539156525252005,
    -1.0925484305920792,
    0.5462742152960396,
)
HARMONIC_THREE = (
    -0.5900435899266435,
    2.890611442640554,
    -0.4570457994644658,
    0.3731763325901154,
    -0.4570457994644658,
    1.445305721320277,
    -0.5900435899266435,
)


def harmonics(east, north, ahead):
    east_east = east * east
    north_north = north * north
    ahead_ahead = ahead * ahead
    terms = [
        jnp.full_like(east, HARMONIC_ZERO),
        -HARMONIC_ONE * north,
        HARMONIC_ONE * ahead,
        -HARMONIC_ONE * east,
        HARMONIC_TWO[0] * east * north,
        HARMONIC_TWO[1] * north * ahead,
        HARMONIC_TWO[2] * (2.0 * ahead_ahead - east_east - north_north),
        HARMONIC_TWO[3] * east * ahead,
        HARMONIC_TWO[4] * (east_east - north_north),
        HARMONIC_THREE[0] * north * (3.0 * east_east - north_north),
        HARMONIC_THREE[1] * east * north * ahead,
        HARMONIC_THREE[2] * north * (4.0 * ahead_ahead - east_east - north_north),
        HARMONIC_THREE[3] * ahead * (2.0 * ahead_ahead - 3.0 * east_east - 3.0 * north_north),
        HARMONIC_THREE[4] * east * (4.0 * ahead_ahead - east_east - north_north),
        HARMONIC_THREE[5] * ahead * (east_east - north_north),
        HARMONIC_THREE[6] * east * (east_east - 3.0 * north_north),
    ]
    return terms


def lane_order():
    order = np.zeros((BLOCK, BLOCK), np.float32)
    for step in range(STEPS):
        for segment in range(SEGMENTS):
            order[STEPS * segment + step, SEGMENTS * step + segment] = 1.0
    return order


def pixel_tables():
    pixel = np.arange(PIXELS)
    across = (pixel % 16) - 7.5
    down = (pixel // 16) - 7.5
    ones = np.ones(PIXELS)
    moments = np.zeros((8, PIXELS), np.float32)
    moments[0:6] = [ones, across, down, across * across, across * down, down * down]
    quadratic = np.zeros((32, PIXELS), np.float32)
    for base in range(6):
        quadratic[3 * base : 3 * base + 3] = moments[base]
    forms = np.zeros((32, 3 * PIXELS), np.float32)
    forms[0:3, :PIXELS] = across
    forms[3:6, :PIXELS] = down
    forms[6:9, :PIXELS] = ones
    forms[9:12, PIXELS : 2 * PIXELS] = down
    forms[12:15, PIXELS : 2 * PIXELS] = ones
    forms[15:18, 2 * PIXELS :] = ones
    return quadratic, forms, moments


def rounded(value):
    return value.astype(jnp.bfloat16).astype(jnp.float32)


def split3(value):
    high = rounded(value)
    rest = value - high
    middle = rounded(rest)
    return high, middle, rest - middle


def split2(value):
    high = rounded(value)
    return high, rounded(value - high)


CONTRACT_ROWS = (((0,), (0,)), ((), ()))
CONTRACT_LANES = (((1,), (1,)), ((), ()))


def blend_kernel(
    pairs_ref, place_ref, arrived_ref, target_ref, quadratic_ref, forms_ref, moments_ref,
    image_ref, grad_ref,
    block_ref, form_ref, tint_ref, center_ref, steep_ref, power_ref, glow_power_ref,
    alpha_ref, weight_ref, trans_ref, local_ref, carry_ref, behind_ref, glow_ref, rows_ref,
    sums_ref,
):
    f32 = jnp.float32
    bf16 = jnp.bfloat16
    tiles = target_ref.shape[1]
    segment = lax.broadcasted_iota(jnp.int32, (SEGMENTS, PIXELS), 0)
    slot_row = lax.broadcasted_iota(jnp.int32, (SLOTS, BLOCK), 0)
    lane_segment = lax.rem(lax.broadcasted_iota(jnp.int32, (SEGMENTS, BLOCK), 1), SEGMENTS)
    own_segment = (lane_segment == lax.broadcasted_iota(jnp.int32, (SEGMENTS, BLOCK), 0)).astype(f32)

    def clear(place, steep):
        grad_ref[place] = jnp.zeros(grad_ref.shape[1:], f32)
        forms = arrived_ref[place, :, 2 * BLOCK : 5 * BLOCK]
        return jnp.maximum(steep, forms * forms)

    steep = lax.fori_loop(0, grad_ref.shape[0], clear, jnp.zeros((1, 3 * BLOCK), f32), unroll=8)
    smooth = (
        jnp.max(steep[:, 0:BLOCK] + steep[:, BLOCK : 2 * BLOCK] + steep[:, 2 * BLOCK : 3 * BLOCK])
        <= SMOOTH_TRACE
    )
    form_ref[...] = jnp.zeros_like(form_ref)
    for empty in (tint_ref, center_ref, rows_ref, glow_ref, carry_ref, behind_ref):
        empty[...] = jnp.zeros_like(empty)
    for bank in range(2):
        rows_ref[bank, 0:8, :] = moments_ref[...]

    def clear_steps(slot, _):
        alpha_ref[1, slot] = jnp.zeros(alpha_ref.shape[2:], f32)
        weight_ref[1, slot] = jnp.zeros(weight_ref.shape[2:], f32)
        return 0

    lax.fori_loop(0, SLOTS, clear_steps, 0)

    def place_of(row, slot):
        return jnp.maximum(pairs_ref[row, slot], 0)

    def prepare(row, bank, quick):
        view = place_ref[row]
        center_x = (16 * lax.rem(view, TX) + 8).astype(f32)
        center_y = (16 * lax.div(view, TX) + 8).astype(f32)
        live = jnp.zeros((SLOTS, BLOCK), f32)
        for slot in range(SLOTS):
            live = jnp.where(slot_row == slot, (pairs_ref[row, slot] >= 0).astype(f32), live)
            place = place_of(row, slot)
            for base in range(9):
                block_ref[16 * slot + base : 16 * slot + base + 1, :] = arrived_ref[
                    place, :, BLOCK * base : BLOCK * base + BLOCK
                ]

        def fetched(base):
            return block_ref[pl.ds(base, SLOTS, stride=16), :]

        across = fetched(0) - center_x
        down = fetched(1) - center_y
        center_ref[bank, 0] = across
        center_ref[bank, 1] = down
        form_xx, form_xy, form_yy = fetched(2), fetched(3), fetched(4)
        log_opacity = jnp.where(live > 0.0, fetched(5), -1e9)
        shift_one = -(form_xx * across + form_xy * down)
        shift_two = -(form_yy * down)
        if quick:
            shift_one = jnp.clip(shift_one, -1e4, 1e4)
            shift_two = jnp.clip(shift_two, -1e4, 1e4)
            values = (
                log_opacity - shift_one * shift_one - shift_two * shift_two,
                -2.0 * (form_xx * shift_one),
                -2.0 * (form_xy * shift_one + form_yy * shift_two),
                -(form_xx * form_xx),
                -2.0 * (form_xx * form_xy),
                -(form_xy * form_xy + form_yy * form_yy),
            )
        else:
            values = (form_xx, form_xy, shift_one, form_yy, shift_two, log_opacity)
        for base, value in enumerate(values):
            for part, piece in enumerate(split3(value)):
                form_ref[pl.ds(8 * (3 * base + part), SLOTS), :] = piece
        for channel in range(3):
            high, low = split2(fetched(6 + channel))
            for base, piece in enumerate((high, low, high)):
                tint_ref[bank, pl.ds(8 * (3 * base + channel), SLOTS), :] = piece

    def exponents(slot, bank, quick):
        lhs = form_ref[pl.ds(slot, 32, stride=8), :].astype(bf16)
        if quick:
            power_ref[bank, slot] = lax.dot_general(
                lhs, quadratic_ref[...], CONTRACT_ROWS, preferred_element_type=f32
            )
            return
        steep_ref[...] = lax.dot_general(lhs, forms_ref[...], CONTRACT_ROWS, preferred_element_type=f32)

    def joined(kept, inner):
        halves = [jnp.concatenate([piece for part in kept[2 * inner + half] for piece in part], axis=0) for half in range(2)]
        return jnp.concatenate(halves, axis=1)

    def ahead(slots, bank, quick):
        chains = [(inner, half) for inner in range(len(slots)) for half in range(2)]
        trans = [jnp.ones((SEGMENTS, 128), f32) for _ in chains]
        kept = [[[None] * (STEPS // 2) for _ in range(2)] for _ in chains]

        def keep(chain, pair, value):
            high = value.astype(bf16)
            kept[chain][0][pair] = high
            kept[chain][1][pair] = (value - high.astype(f32)).astype(bf16)

        for pair in range(STEPS // 2):
            weights = [[] for _ in chains]
            for step in (2 * pair, 2 * pair + 1):
                eight = slice(8 * step, 8 * step + 8)
                for chain, (inner, half) in enumerate(chains):
                    lanes = slice(128 * half, 128 * half + 128)
                    if quick:
                        exponent = jnp.minimum(power_ref[bank, slots[inner], eight, lanes], 0.0)
                    else:
                        one = steep_ref[eight, lanes]
                        two = steep_ref[eight, 256 + 128 * half : 384 + 128 * half]
                        three = steep_ref[eight, 512 + 128 * half : 640 + 128 * half]
                        exponent = three - one * one - two * two
                    alpha = jnp.exp2(exponent)
                    weight = alpha * trans[chain]
                    trans[chain] = trans[chain] - weight
                    alpha_ref[bank, slots[inner], eight, lanes] = alpha
                    weight_ref[bank, slots[inner], eight, lanes] = weight
                    weights[chain].append(weight)
            for chain in range(len(chains)):
                keep(chain, pair, jnp.concatenate(weights[chain], axis=0))
        for chain, (inner, half) in enumerate(chains):
            trans_ref[slots[inner], :, 128 * half : 128 * half + 128] = trans[chain]
        for inner, slot in enumerate(slots):
            parts = [own_segment * tint_ref[bank, pl.ds(8 * base + slot, 1), :] for base in range(6)]
            lhs = jnp.concatenate(parts, axis=0).astype(bf16)
            found = lax.dot_general(
                jnp.concatenate([lhs, lhs], axis=1), joined(kept, inner),
                (((1,), (0,)), ((), ())), preferred_element_type=f32,
            )
            local_ref[slot] = found[0:24] + found[24:48]

    def middle(row, bank):
        before = jnp.ones((1, PIXELS), f32)
        seen = [jnp.zeros((SEGMENTS, PIXELS), f32) for _ in range(3)]
        for slot in range(SLOTS):
            through = trans_ref[slot]
            for reach in (1, 2, 4):
                through = through * jnp.where(segment >= reach, pltpu.roll(through, reach, 0), 1.0)
            carry = jnp.where(segment >= 1, pltpu.roll(through, 1, 0), 1.0) * before
            carry_ref[bank, slot] = carry
            for channel in range(3):
                seen[channel] = seen[channel] + carry * local_ref[slot, 8 * channel : 8 * channel + 8, :]
            before = before * through[7:8]
        glow = []
        for channel in range(3):
            color = jnp.sum(seen[channel], axis=0, keepdims=True)
            image_ref[channel, pl.ds(row, 1), :] = color
            value = (color - target_ref[channel, pl.ds(row, 1), :]) * (2.0 / 512.0)
            glow.append(value)
            high, low = split2(value)
            for base, piece in enumerate((high, high, low)):
                glow_ref[bank, 3 * base + channel : 3 * base + channel + 1, :] = piece
            rows_ref[bank, 8 + channel : 9 + channel, :] = high
            rows_ref[bank, 16 + channel : 17 + channel, :] = low

        after = jnp.zeros((1, PIXELS), f32)
        for slot in reversed(range(SLOTS)):
            through = trans_ref[slot]
            light = (
                local_ref[slot, 0:8, :] * glow[0]
                + local_ref[slot, 8:16, :] * glow[1]
                + local_ref[slot, 16:24, :] * glow[2]
            )
            for reach in (1, 2, 4):
                inside = segment < SEGMENTS - reach
                light = light + through * jnp.where(inside, pltpu.roll(light, SEGMENTS - reach, 0), 0.0)
                through = through * jnp.where(inside, pltpu.roll(through, SEGMENTS - reach, 0), 1.0)
            start = light + through * after
            behind_ref[bank, slot] = jnp.where(segment < SEGMENTS - 1, pltpu.roll(start, SEGMENTS - 1, 0), after)
            after = start[0:1]

    def glows(slot, bank):
        glow_power_ref[bank, slot] = lax.dot_general(
            tint_ref[bank, pl.ds(slot, 16, stride=8), :].astype(bf16), glow_ref[bank].astype(bf16),
            CONTRACT_ROWS, preferred_element_type=f32,
        )

    def back(slots, bank):
        chains = [(inner, half) for inner in range(len(slots)) for half in range(2)]
        behind = [behind_ref[bank, slots[inner], :, 128 * half : 128 * half + 128] for inner, half in chains]
        kept = [[[None] * (STEPS // 2) for _ in range(4)] for _ in chains]
        for pair in reversed(range(STEPS // 2)):
            pulls = [[] for _ in chains]
            weights = [[] for _ in chains]
            for step in (2 * pair + 1, 2 * pair):
                eight = slice(8 * step, 8 * step + 8)
                for chain, (inner, half) in enumerate(chains):
                    lanes = slice(128 * half, 128 * half + 128)
                    alpha = alpha_ref[bank, slots[inner], eight, lanes]
                    carry = carry_ref[bank, slots[inner], :, lanes]
                    weight = weight_ref[bank, slots[inner], eight, lanes] * carry
                    gain = glow_power_ref[bank, slots[inner], eight, lanes] - behind[chain]
                    behind[chain] = behind[chain] + alpha * gain
                    pulls[chain].append(weight * gain)
                    weights[chain].append(weight)
            for chain in range(len(chains)):
                for base, parts in ((0, pulls[chain]), (2, weights[chain])):
                    value = jnp.concatenate([parts[1], parts[0]], axis=0)
                    high = value.astype(bf16)
                    kept[chain][base][pair] = high
                    kept[chain][base + 1][pair] = (value - high.astype(f32)).astype(bf16)
        lhs_rows = rows_ref[bank].astype(bf16)
        for inner, slot in enumerate(slots):
            found = lax.dot_general(
                lhs_rows, joined(kept, inner), CONTRACT_LANES, preferred_element_type=f32
            )
            tints = found[8:24, 256:384] + found[8:24, 384:512]
            sums_ref[pl.ds(16 * slot, 8), :] = found[0:8, 0:128] + found[0:8, 128:256]
            sums_ref[pl.ds(16 * slot + 8, 8), :] = tints[0:8] + tints[8:16]

    def finish(row, bank):
        across = center_ref[bank, 0]
        down = center_ref[bank, 1]

        def summed(base):
            return sums_ref[pl.ds(base, SLOTS, stride=16), :]

        total, sum_x, sum_y = summed(0), summed(1), summed(2)
        off_x = sum_x - across * total
        off_y = sum_y - down * total
        sum_xx = summed(3) - across * (sum_x + off_x)
        sum_xy = summed(4) - across * sum_y - down * off_x
        sum_yy = summed(5) - down * (sum_y + off_y)
        values = (off_x, off_y, sum_xx, sum_xy, sum_yy, total, summed(8), summed(9), summed(10))
        for base, value in enumerate(values):
            sums_ref[pl.ds(base, SLOTS, stride=16), :] = value
        for slot in range(SLOTS):
            place = place_of(row, slot)
            for base in range(9):
                lanes = slice(BLOCK * base, BLOCK * base + BLOCK)
                grad_ref[place, :, lanes] = (
                    grad_ref[place, :, lanes] + sums_ref[16 * slot + base : 16 * slot + base + 1, :]
                )

    groups = [list(range(first, first + GROUP)) for first in range(0, SLOTS, GROUP)]

    def both(row, bank):
        prepare(row, bank, True)
        for slot in range(SLOTS):
            exponents(slot, bank, True)
            glows(slot, 1 - bank)
        for group in groups:
            ahead(group, bank, True)
            back(group, 1 - bank)
        finish(jnp.maximum(row - 1, 0), 1 - bank)
        middle(row, bank)

    @pl.when(smooth)
    def _():
        def two(pair, _):
            both(2 * pair, 0)
            both(2 * pair + 1, 1)
            return 0

        lax.fori_loop(0, tiles // 2, two, 0)
        for slot in range(SLOTS):
            glows(slot, 1)
        for group in groups:
            back(group, 1)
        finish(tiles - 1, 1)

    @pl.when(jnp.logical_not(smooth))
    def _():
        def tile(row, _):
            def forth(slot, _):
                exponents(slot, 0, False)
                ahead([slot], 0, False)
                return 0

            def back_one(slot, _):
                glows(slot, 0)
                back([slot], 0)
                return 0

            prepare(row, 0, False)
            lax.fori_loop(0, SLOTS, forth, 0)
            middle(row, 0)
            lax.fori_loop(0, SLOTS, back_one, 0)
            finish(row, 0)
            return 0

        lax.fori_loop(0, tiles, tile, 0)


def blend(pairs, tile_place, arrived, target):
    quadratic, forms, moments = pixel_tables()
    tiles = target.shape[1]
    f32 = jnp.float32
    bf16 = jnp.bfloat16
    vmem = pl.BlockSpec(memory_space=pltpu.VMEM)
    smem = pl.BlockSpec(memory_space=pltpu.SMEM)
    return pl.pallas_call(
        blend_kernel,
        out_shape=(
            jax.ShapeDtypeStruct((3, tiles, PIXELS), f32),
            jax.ShapeDtypeStruct(arrived.shape, f32),
        ),
        in_specs=[smem, smem, vmem, vmem, vmem, vmem, vmem],
        out_specs=(vmem, vmem),
        scratch_shapes=[
            pltpu.VMEM((SLOTS * 16, BLOCK), f32),
            pltpu.VMEM((32 * SLOTS, BLOCK), f32),
            pltpu.VMEM((2, 16 * SLOTS, BLOCK), f32),
            pltpu.VMEM((2, 2, SLOTS, BLOCK), f32),
            pltpu.VMEM((BLOCK, 3 * PIXELS), f32),
            pltpu.VMEM((2, SLOTS, BLOCK, PIXELS), f32),
            pltpu.VMEM((2, SLOTS, BLOCK, PIXELS), f32),
            pltpu.VMEM((2, SLOTS, BLOCK, PIXELS), f32),
            pltpu.VMEM((2, SLOTS, BLOCK, PIXELS), f32),
            pltpu.VMEM((SLOTS, SEGMENTS, PIXELS), f32),
            pltpu.VMEM((SLOTS, 3 * SEGMENTS, PIXELS), f32),
            pltpu.VMEM((2, SLOTS, SEGMENTS, PIXELS), f32),
            pltpu.VMEM((2, SLOTS, SEGMENTS, PIXELS), f32),
            pltpu.VMEM((2, 16, PIXELS), f32),
            pltpu.VMEM((2, 32, PIXELS), f32),
            pltpu.VMEM((SLOTS * 16, BLOCK), f32),
        ],
        compiler_params=pltpu.CompilerParams(vmem_limit_bytes=24 << 20),
        cost_estimate=pl.CostEstimate(flops=200_000_000, bytes_accessed=6_000_000, transcendentals=4_000_000),
        name="blend",
    )(
        pairs, tile_place, arrived, target, jnp.asarray(quadratic, bf16),
        jnp.asarray(forms, bf16), jnp.asarray(moments, f32),
    )


def screen_of(raw, width, height):
    place_x, place_y, place_z = raw[0], raw[1], raw[2]
    screen_u = width * place_x / place_z + 0.5 * width
    screen_v = width * place_y / place_z + 0.5 * height
    inverse_one = jnp.exp(-2.0 * raw[3])
    inverse_two = jnp.exp(-2.0 * raw[4])
    cosine = jnp.cos(raw[5])
    sine = jnp.sin(raw[5])
    conic_a = cosine * cosine * inverse_one + sine * sine * inverse_two
    conic_b = cosine * sine * (inverse_one - inverse_two)
    conic_c = sine * sine * inverse_one + cosine * cosine * inverse_two
    log_opacity = jnp.minimum(raw[6], 0.0) - jnp.log1p(jnp.exp(-jnp.abs(raw[6])))
    length = jnp.sqrt(place_x * place_x + place_y * place_y + place_z * place_z)
    basis = harmonics(place_x / length, place_y / length, place_z / length)
    colors = []
    for channel in range(3):
        color = raw[7 + 16 * channel] * basis[0]
        for term in range(1, 16):
            color = color + raw[7 + 16 * channel + term] * basis[term]
        colors.append(0.5 + color)
    return [screen_u, screen_v, conic_a, conic_b, conic_c, log_opacity] + colors


def permuted(value, order):
    high, middle, low = (part.astype(jnp.bfloat16) for part in split3(value))
    rows = value.shape[0]
    found = jnp.dot(jnp.concatenate([high, middle, low], axis=0), order, preferred_element_type=jnp.float32)
    return found[0:rows] + found[rows : 2 * rows] + found[2 * rows : 3 * rows]


def project_kernel(width, height, splats_ref, order_ref, rows_ref):
    params, blocks, _ = splats_ref.shape
    raw = [splats_ref[base] for base in range(params)]
    found = screen_of(raw, width, height)
    conic_a, conic_b, conic_c = found[2:5]
    steep = conic_a > 1e-30
    over = lax.rsqrt(jnp.where(steep, conic_a, 1.0))
    form_xx = jnp.sqrt(conic_a)
    form_xy = jnp.where(steep, conic_b * over, 0.0)
    form_yy = jnp.where(steep, jnp.exp(-raw[3] - raw[4]) * over, jnp.sqrt(conic_c))
    rows = [found[0], found[1], FORM_SCALE * form_xx, FORM_SCALE * form_xy, FORM_SCALE * form_yy, LOG2_E * found[5]]
    for base, value in enumerate(rows + found[6:9]):
        value = permuted(value, order_ref[...])
        for block in range(blocks):
            rows_ref[block, :, BLOCK * base : BLOCK * base + BLOCK] = value[block : block + 1, :]


def project(splats, width, height):
    _, blocks, lanes = splats.shape
    vmem = pl.BlockSpec(memory_space=pltpu.VMEM)
    return pl.pallas_call(
        functools.partial(project_kernel, width, height),
        out_shape=jax.ShapeDtypeStruct((blocks, 1, 9 * lanes), jnp.float32),
        in_specs=[vmem, vmem],
        out_specs=vmem,
        cost_estimate=pl.CostEstimate(flops=5_000_000, bytes_accessed=1_000_000, transcendentals=30_000),
        compiler_params=pltpu.CompilerParams(vmem_limit_bytes=8 << 20),
        name="project",
    )(splats, jnp.asarray(lane_order(), jnp.bfloat16))


def asked_parts(held_ref, asked_ref, sem):
    share = held_ref.shape[0] // PARTS
    copies = []
    for part in range(PARTS):
        owners = pl.ds(part * share, share)
        copies.append(pltpu.make_async_copy(held_ref.at[owners], asked_ref.at[owners], sem.at[part]))
        copies[-1].start()
    return copies


def pack_kernel(held_ref, rows_ref, payload_ref, asked_ref, staged_ref, sem, asked_sem):
    owners, _, most = asked_ref.shape
    share = owners // PARTS
    asked_copies = asked_parts(held_ref, asked_ref, asked_sem)
    copies = []
    for part in range(PARTS):
        asked_copies[part].wait()

        def one(step, _, first=part * share):
            owner = first + step
            for which in range(most):
                staged_ref[owner * most + which] = rows_ref[jnp.maximum(asked_ref[owner, 0, which], 0)]
            return 0

        lax.fori_loop(0, share, one, 0, unroll=8)
        places = pl.ds(part * share * most, share * most)
        copies.append(pltpu.make_async_copy(staged_ref.at[places], payload_ref.at[places], sem.at[part]))
        copies[-1].start()
    for copy in copies:
        copy.wait()


def pack(asked, rows):
    vmem = pl.BlockSpec(memory_space=pltpu.VMEM)
    return pl.pallas_call(
        pack_kernel,
        out_shape=jax.ShapeDtypeStruct((asked.shape[0] * asked.shape[2],) + rows.shape[1:], jnp.float32),
        in_specs=[vmem, vmem],
        out_specs=pl.BlockSpec(memory_space=pl.ANY),
        scratch_shapes=[
            pltpu.SMEM(asked.shape, jnp.int32),
            pltpu.VMEM((asked.shape[0] * asked.shape[2],) + rows.shape[1:], jnp.float32),
            pltpu.SemaphoreType.DMA((PARTS,)),
            pltpu.SemaphoreType.DMA((PARTS,)),
        ],
        cost_estimate=pl.CostEstimate(flops=0, bytes_accessed=2_000_000, transcendentals=0),
        compiler_params=pltpu.CompilerParams(vmem_limit_bytes=8 << 20),
        name="pack",
    )(asked, rows)


def update_kernel(
    width, height, held_ref, returned_ref, splats_ref, one_ref, two_ref, order_ref,
    grad_out_ref, step_out_ref, asked_ref, asked_sem, grad_ref, step_ref, sem, sum_ref, rows_ref,
    pulled_ref, *lane_refs,
):
    params, blocks, _ = splats_ref.shape
    asked_copies = asked_parts(held_ref, asked_ref, asked_sem)
    for lane_ref in lane_refs:
        lane_ref[...] = jnp.zeros_like(lane_ref)

    owners, _, most = asked_ref.shape
    step = len(lane_refs) // most

    def gather(group, _):
        for lane, lane_ref in enumerate(lane_refs):
            block = jnp.maximum(asked_ref[group * step + lane // most, 0, lane % most], 0)
            lane_ref[block] = lane_ref[block] + returned_ref[group * len(lane_refs) + lane]
        return 0

    share = owners // step // PARTS
    for part in range(PARTS):
        asked_copies[part].wait()
        lax.fori_loop(part * share, part * share + share, gather, 0, unroll=2)
    for block in range(blocks):
        value = lane_refs[0][block]
        for lane_ref in lane_refs[1:]:
            value = value + lane_ref[block]
        sum_ref[block] = value
        for base in range(9):
            rows_ref[blocks * base + block : blocks * base + block + 1, :] = sum_ref[
                block, :, BLOCK * base : BLOCK * base + BLOCK
            ]
    pulled_ref[...] = permuted(rows_ref[...], order_ref[...])
    copies = []
    for first in range(0, blocks, 8):
        eight = slice(first, first + 8)
        raw = [splats_ref[base, eight, :] for base in range(params)]
        summed = [pulled_ref[blocks * base + first : blocks * base + first + 8, :] for base in range(9)]
        found, pull = jax.vjp(functools.partial(screen_of, width=width, height=height), raw)
        conic_a, conic_b, conic_c = found[2:5]
        (pulled,) = pull(
            [
                conic_a * summed[0] + conic_b * summed[1],
                conic_b * summed[0] + conic_c * summed[1],
                -0.5 * summed[2],
                -summed[3],
                -0.5 * summed[4],
                summed[5],
            ]
            + summed[6:9]
        )
        for base, grad in enumerate(pulled):
            grad_ref[base, eight, :] = grad
            moved = 0.9 * one_ref[base, eight, :] + 0.1 * grad
            second = 0.999 * two_ref[base, eight, :] + 0.001 * grad * grad
            step_ref[base, eight, :] = moved / (jnp.sqrt(second) + 1e-08)
        for which, (held, out) in enumerate(((grad_ref, grad_out_ref), (step_ref, step_out_ref))):
            copies.append(
                pltpu.make_async_copy(
                    held.at[:, pl.ds(first, 8), :], out.at[:, pl.ds(first, 8), :], sem.at[first // 8, which]
                )
            )
            copies[-1].start()
    for copy in copies:
        copy.wait()


def update(asked, returned, splats, moment_one, moment_two, width, height):
    params, blocks, lanes = splats.shape
    vmem = pl.BlockSpec(memory_space=pltpu.VMEM)
    f32 = jnp.float32
    shape = jax.ShapeDtypeStruct(splats.shape, f32)
    row_sums = pltpu.VMEM((blocks, 1, 9 * lanes), f32)
    return pl.pallas_call(
        functools.partial(update_kernel, width, height),
        out_shape=(shape, shape),
        in_specs=[vmem] * 6,
        out_specs=(pl.BlockSpec(memory_space=pl.ANY), pl.BlockSpec(memory_space=pl.ANY)),
        scratch_shapes=[
            pltpu.SMEM(asked.shape, jnp.int32),
            pltpu.SemaphoreType.DMA((PARTS,)),
            pltpu.VMEM(splats.shape, f32),
            pltpu.VMEM(splats.shape, f32),
            pltpu.SemaphoreType.DMA((blocks // 8, 2)),
            row_sums,
            pltpu.VMEM((9 * blocks, lanes), f32),
            pltpu.VMEM((9 * blocks, lanes), f32),
        ]
        + [row_sums] * 8,
        cost_estimate=pl.CostEstimate(flops=8_000_000, bytes_accessed=6_000_000, transcendentals=500_000),
        compiler_params=pltpu.CompilerParams(vmem_limit_bytes=16 << 20),
        name="update",
    )(asked, returned, splats, moment_one, moment_two, jnp.asarray(lane_order().T, jnp.bfloat16))


def trade(payload):
    return lax.all_to_all(payload, ("gx", "gy"), split_axis=0, concat_axis=0, tiled=True)


def local(splats, moment_one, moment_two, target, tile_place, pairs, fetch):
    devices = lax.axis_size("gx") * lax.axis_size("gy")
    tiles_here = target.shape[0]
    width = 16.0 * TX
    height = 16.0 * (tiles_here * devices // TX)
    flat, first_moment, second_moment = (
        jnp.transpose(value, (1, 0, 2)) for value in (splats, moment_one, moment_two)
    )
    asked = trade(fetch.reshape(fetch.shape[1], 1, fetch.shape[2]))
    rows = project(flat, width, height)
    arrived = trade(pack(asked, rows))
    image, received = blend(pairs, tile_place, arrived, jnp.transpose(target, (1, 0, 2)))
    grad, step = update(asked, trade(received), flat, first_moment, second_moment, width, height)
    return tuple(jnp.transpose(value, (1, 0, 2)) for value in (image, grad, step))


def solution(mesh):
    return jax.shard_map(
        local,
        mesh=mesh,
        in_specs=(
            P(("gx", "gy"), None, None),
            P(("gx", "gy"), None, None),
            P(("gx", "gy"), None, None),
            P(("gx", "gy"), None, None),
            P(("gx", "gy")),
            P(("gx", "gy"), None),
            P(("gx", "gy"), None, None),
        ),
        out_specs=(
            P(("gx", "gy"), None, None),
            P(("gx", "gy"), None, None),
            P(("gx", "gy"), None, None),
        ),
        check_vma=False,
    )
```

```python
import functools

import jax
import jax.numpy as jnp
import numpy as np
from jax import lax
from jax.experimental import pallas as pl
from jax.experimental.pallas import tpu as pltpu
from jax.sharding import PartitionSpec as P

TX = 16
BLOCK = 128
SEGMENTS = 8
STEPS = BLOCK // SEGMENTS
SLOTS = 8
PIXELS = 256
LOG2_E = 1.4426950408889634
FORM_SCALE = 0.8493218002880191
SMOOTH_TRACE = 0.75
GROUP = 2
PARTS = 4

HARMONIC_ZERO = 0.28209479177387814
HARMONIC_ONE = 0.4886025119029199
HARMONIC_TWO = (
    1.0925484305920792,
    -1.0925484305920792,
    0.31539156525252005,
    -1.0925484305920792,
    0.5462742152960396,
)
HARMONIC_THREE = (
    -0.5900435899266435,
    2.890611442640554,
    -0.4570457994644658,
    0.3731763325901154,
    -0.4570457994644658,
    1.445305721320277,
    -0.5900435899266435,
)


def harmonics(east, north, ahead):
    east_east = east * east
    north_north = north * north
    ahead_ahead = ahead * ahead
    terms = [
        jnp.full_like(east, HARMONIC_ZERO),
        -HARMONIC_ONE * north,
        HARMONIC_ONE * ahead,
        -HARMONIC_ONE * east,
        HARMONIC_TWO[0] * east * north,
        HARMONIC_TWO[1] * north * ahead,
        HARMONIC_TWO[2] * (2.0 * ahead_ahead - east_east - north_north),
        HARMONIC_TWO[3] * east * ahead,
        HARMONIC_TWO[4] * (east_east - north_north),
        HARMONIC_THREE[0] * north * (3.0 * east_east - north_north),
        HARMONIC_THREE[1] * east * north * ahead,
        HARMONIC_THREE[2] * north * (4.0 * ahead_ahead - east_east - north_north),
        HARMONIC_THREE[3] * ahead * (2.0 * ahead_ahead - 3.0 * east_east - 3.0 * north_north),
        HARMONIC_THREE[4] * east * (4.0 * ahead_ahead - east_east - north_north),
        HARMONIC_THREE[5] * ahead * (east_east - north_north),
        HARMONIC_THREE[6] * east * (east_east - 3.0 * north_north),
    ]
    return terms


def lane_order():
    order = np.zeros((BLOCK, BLOCK), np.float32)
    for step in range(STEPS):
        for segment in range(SEGMENTS):
            order[STEPS * segment + step, SEGMENTS * step + segment] = 1.0
    return order


def pixel_tables():
    pixel = np.arange(PIXELS)
    across = (pixel % 16) - 7.5
    down = (pixel // 16) - 7.5
    ones = np.ones(PIXELS)
    moments = np.zeros((8, PIXELS), np.float32)
    moments[0:6] = [ones, across, down, across * across, across * down, down * down]
    quadratic = np.zeros((32, PIXELS), np.float32)
    for base in range(6):
        quadratic[3 * base : 3 * base + 3] = moments[base]
    forms = np.zeros((32, 3 * PIXELS), np.float32)
    forms[0:3, :PIXELS] = across
    forms[3:6, :PIXELS] = down
    forms[6:9, :PIXELS] = ones
    forms[9:12, PIXELS : 2 * PIXELS] = down
    forms[12:15, PIXELS : 2 * PIXELS] = ones
    forms[15:18, 2 * PIXELS :] = ones
    return quadratic, forms, moments


def rounded(value):
    return value.astype(jnp.bfloat16).astype(jnp.float32)


def split3(value):
    high = rounded(value)
    rest = value - high
    middle = rounded(rest)
    return high, middle, rest - middle


def split2(value):
    high = rounded(value)
    return high, rounded(value - high)


CONTRACT_ROWS = (((0,), (0,)), ((), ()))
CONTRACT_LANES = (((1,), (1,)), ((), ()))


def blend_kernel(
    pairs_ref, place_ref, arrived_ref, target_ref, quadratic_ref, forms_ref, moments_ref,
    image_ref, grad_ref,
    block_ref, form_ref, tint_ref, center_ref, steep_ref, power_ref, glow_power_ref,
    alpha_ref, weight_ref, trans_ref, local_ref, carry_ref, behind_ref, glow_ref, rows_ref,
    sums_ref,
):
    f32 = jnp.float32
    bf16 = jnp.bfloat16
    tiles = target_ref.shape[1]
    segment = lax.broadcasted_iota(jnp.int32, (SEGMENTS, PIXELS), 0)
    slot_row = lax.broadcasted_iota(jnp.int32, (SLOTS, BLOCK), 0)
    lane_segment = lax.rem(lax.broadcasted_iota(jnp.int32, (SEGMENTS, BLOCK), 1), SEGMENTS)
    own_segment = (lane_segment == lax.broadcasted_iota(jnp.int32, (SEGMENTS, BLOCK), 0)).astype(f32)

    def clear(place, steep):
        grad_ref[place] = jnp.zeros(grad_ref.shape[1:], f32)
        forms = arrived_ref[place, :, 2 * BLOCK : 5 * BLOCK]
        return jnp.maximum(steep, forms * forms)

    steep = lax.fori_loop(0, grad_ref.shape[0], clear, jnp.zeros((1, 3 * BLOCK), f32), unroll=8)
    smooth = (
        jnp.max(steep[:, 0:BLOCK] + steep[:, BLOCK : 2 * BLOCK] + steep[:, 2 * BLOCK : 3 * BLOCK])
        <= SMOOTH_TRACE
    )
    form_ref[...] = jnp.zeros_like(form_ref)
    for empty in (tint_ref, center_ref, rows_ref, glow_ref, carry_ref, behind_ref):
        empty[...] = jnp.zeros_like(empty)
    for bank in range(2):
        rows_ref[bank, 0:8, :] = moments_ref[...]

    def clear_steps(slot, _):
        alpha_ref[1, slot] = jnp.zeros(alpha_ref.shape[2:], f32)
        weight_ref[1, slot] = jnp.zeros(weight_ref.shape[2:], f32)
        return 0

    lax.fori_loop(0, SLOTS, clear_steps, 0)

    def place_of(row, slot):
        return jnp.maximum(pairs_ref[slot, row], 0)

    def prepare(row, bank, quick):
        view = place_ref[row]
        center_x = (16 * lax.rem(view, TX) + 8).astype(f32)
        center_y = (16 * lax.div(view, TX) + 8).astype(f32)
        live = jnp.zeros((SLOTS, BLOCK), f32)
        for slot in range(SLOTS):
            live = jnp.where(slot_row == slot, (pairs_ref[slot, row] >= 0).astype(f32), live)
            place = place_of(row, slot)
            for base in range(9):
                block_ref[16 * slot + base : 16 * slot + base + 1, :] = arrived_ref[
                    place, :, BLOCK * base : BLOCK * base + BLOCK
                ]

        def fetched(base):
            return block_ref[pl.ds(base, SLOTS, stride=16), :]

        across = fetched(0) - center_x
        down = fetched(1) - center_y
        center_ref[bank, 0] = across
        center_ref[bank, 1] = down
        form_xx, form_xy, form_yy = fetched(2), fetched(3), fetched(4)
        log_opacity = jnp.where(live > 0.0, fetched(5), -1e9)
        shift_one = -(form_xx * across + form_xy * down)
        shift_two = -(form_yy * down)
        if quick:
            shift_one = jnp.clip(shift_one, -1e4, 1e4)
            shift_two = jnp.clip(shift_two, -1e4, 1e4)
            values = (
                log_opacity - shift_one * shift_one - shift_two * shift_two,
                -2.0 * (form_xx * shift_one),
                -2.0 * (form_xy * shift_one + form_yy * shift_two),
                -(form_xx * form_xx),
                -2.0 * (form_xx * form_xy),
                -(form_xy * form_xy + form_yy * form_yy),
            )
        else:
            values = (form_xx, form_xy, shift_one, form_yy, shift_two, log_opacity)
        for base, value in enumerate(values):
            for part, piece in enumerate(split3(value)):
                form_ref[pl.ds(8 * (3 * base + part), SLOTS), :] = piece
        for channel in range(3):
            high, low = split2(fetched(6 + channel))
            for base, piece in enumerate((high, low, high)):
                tint_ref[bank, pl.ds(8 * (3 * base + channel), SLOTS), :] = piece

    def exponents(slot, bank, quick):
        lhs = form_ref[pl.ds(slot, 32, stride=8), :].astype(bf16)
        if quick:
            power_ref[bank, slot] = lax.dot_general(
                lhs, quadratic_ref[...], CONTRACT_ROWS, preferred_element_type=f32
            )
            return
        steep_ref[...] = lax.dot_general(lhs, forms_ref[...], CONTRACT_ROWS, preferred_element_type=f32)

    def joined(kept, inner):
        halves = [jnp.concatenate([piece for part in kept[2 * inner + half] for piece in part], axis=0) for half in range(2)]
        return jnp.concatenate(halves, axis=1)

    def ahead(slots, bank, quick):
        chains = [(inner, half) for inner in range(len(slots)) for half in range(2)]
        trans = [jnp.ones((SEGMENTS, 128), f32) for _ in chains]
        kept = [[[None] * (STEPS // 2) for _ in range(2)] for _ in chains]

        def keep(chain, pair, value):
            high = value.astype(bf16)
            kept[chain][0][pair] = high
            kept[chain][1][pair] = (value - high.astype(f32)).astype(bf16)

        for pair in range(STEPS // 2):
            weights = [[] for _ in chains]
            for step in (2 * pair, 2 * pair + 1):
                eight = slice(8 * step, 8 * step + 8)
                for chain, (inner, half) in enumerate(chains):
                    lanes = slice(128 * half, 128 * half + 128)
                    if quick:
                        exponent = jnp.minimum(power_ref[bank, slots[inner], eight, lanes], 0.0)
                    else:
                        one = steep_ref[eight, lanes]
                        two = steep_ref[eight, 256 + 128 * half : 384 + 128 * half]
                        three = steep_ref[eight, 512 + 128 * half : 640 + 128 * half]
                        exponent = three - one * one - two * two
                    alpha = jnp.exp2(exponent)
                    weight = alpha * trans[chain]
                    trans[chain] = trans[chain] - weight
                    alpha_ref[bank, slots[inner], eight, lanes] = alpha
                    weight_ref[bank, slots[inner], eight, lanes] = weight
                    weights[chain].append(weight)
            for chain in range(len(chains)):
                keep(chain, pair, jnp.concatenate(weights[chain], axis=0))
        for chain, (inner, half) in enumerate(chains):
            trans_ref[slots[inner], :, 128 * half : 128 * half + 128] = trans[chain]
        for inner, slot in enumerate(slots):
            parts = [own_segment * tint_ref[bank, pl.ds(8 * base + slot, 1), :] for base in range(6)]
            lhs = jnp.concatenate(parts, axis=0).astype(bf16)
            found = lax.dot_general(
                jnp.concatenate([lhs, lhs], axis=1), joined(kept, inner),
                (((1,), (0,)), ((), ())), preferred_element_type=f32,
            )
            local_ref[slot] = found[0:24] + found[24:48]

    def middle(row, bank):
        before = jnp.ones((1, PIXELS), f32)
        seen = [jnp.zeros((SEGMENTS, PIXELS), f32) for _ in range(3)]
        for slot in range(SLOTS):
            through = trans_ref[slot]
            for reach in (1, 2, 4):
                through = through * jnp.where(segment >= reach, pltpu.roll(through, reach, 0), 1.0)
            carry = jnp.where(segment >= 1, pltpu.roll(through, 1, 0), 1.0) * before
            carry_ref[bank, slot] = carry
            for channel in range(3):
                seen[channel] = seen[channel] + carry * local_ref[slot, 8 * channel : 8 * channel + 8, :]
            before = before * through[7:8]
        glow = []
        for channel in range(3):
            color = jnp.sum(seen[channel], axis=0, keepdims=True)
            image_ref[channel, pl.ds(row, 1), :] = color
            value = (color - target_ref[channel, pl.ds(row, 1), :]) * (2.0 / 512.0)
            glow.append(value)
            high, low = split2(value)
            for base, piece in enumerate((high, high, low)):
                glow_ref[bank, 3 * base + channel : 3 * base + channel + 1, :] = piece
            rows_ref[bank, 8 + channel : 9 + channel, :] = high
            rows_ref[bank, 16 + channel : 17 + channel, :] = low

        after = jnp.zeros((1, PIXELS), f32)
        for slot in reversed(range(SLOTS)):
            through = trans_ref[slot]
            light = (
                local_ref[slot, 0:8, :] * glow[0]
                + local_ref[slot, 8:16, :] * glow[1]
                + local_ref[slot, 16:24, :] * glow[2]
            )
            for reach in (1, 2, 4):
                inside = segment < SEGMENTS - reach
                light = light + through * jnp.where(inside, pltpu.roll(light, SEGMENTS - reach, 0), 0.0)
                through = through * jnp.where(inside, pltpu.roll(through, SEGMENTS - reach, 0), 1.0)
            start = light + through * after
            behind_ref[bank, slot] = jnp.where(segment < SEGMENTS - 1, pltpu.roll(start, SEGMENTS - 1, 0), after)
            after = start[0:1]

    def glows(slot, bank):
        glow_power_ref[bank, slot] = lax.dot_general(
            tint_ref[bank, pl.ds(slot, 16, stride=8), :].astype(bf16), glow_ref[bank].astype(bf16),
            CONTRACT_ROWS, preferred_element_type=f32,
        )

    def back(slots, bank):
        chains = [(inner, half) for inner in range(len(slots)) for half in range(2)]
        behind = [behind_ref[bank, slots[inner], :, 128 * half : 128 * half + 128] for inner, half in chains]
        kept = [[[None] * (STEPS // 2) for _ in range(4)] for _ in chains]
        for pair in reversed(range(STEPS // 2)):
            pulls = [[] for _ in chains]
            weights = [[] for _ in chains]
            for step in (2 * pair + 1, 2 * pair):
                eight = slice(8 * step, 8 * step + 8)
                for chain, (inner, half) in enumerate(chains):
                    lanes = slice(128 * half, 128 * half + 128)
                    alpha = alpha_ref[bank, slots[inner], eight, lanes]
                    carry = carry_ref[bank, slots[inner], :, lanes]
                    weight = weight_ref[bank, slots[inner], eight, lanes] * carry
                    gain = glow_power_ref[bank, slots[inner], eight, lanes] - behind[chain]
                    behind[chain] = behind[chain] + alpha * gain
                    pulls[chain].append(weight * gain)
                    weights[chain].append(weight)
            for chain in range(len(chains)):
                for base, parts in ((0, pulls[chain]), (2, weights[chain])):
                    value = jnp.concatenate([parts[1], parts[0]], axis=0)
                    high = value.astype(bf16)
                    kept[chain][base][pair] = high
                    kept[chain][base + 1][pair] = (value - high.astype(f32)).astype(bf16)
        lhs_rows = rows_ref[bank].astype(bf16)
        for inner, slot in enumerate(slots):
            found = lax.dot_general(
                lhs_rows, joined(kept, inner), CONTRACT_LANES, preferred_element_type=f32
            )
            tints = found[8:24, 256:384] + found[8:24, 384:512]
            sums_ref[pl.ds(16 * slot, 8), :] = found[0:8, 0:128] + found[0:8, 128:256]
            sums_ref[pl.ds(16 * slot + 8, 8), :] = tints[0:8] + tints[8:16]

    def finish(row, bank):
        across = center_ref[bank, 0]
        down = center_ref[bank, 1]

        def summed(base):
            return sums_ref[pl.ds(base, SLOTS, stride=16), :]

        total, sum_x, sum_y = summed(0), summed(1), summed(2)
        off_x = sum_x - across * total
        off_y = sum_y - down * total
        sum_xx = summed(3) - across * (sum_x + off_x)
        sum_xy = summed(4) - across * sum_y - down * off_x
        sum_yy = summed(5) - down * (sum_y + off_y)
        values = (off_x, off_y, sum_xx, sum_xy, sum_yy, total, summed(8), summed(9), summed(10))
        for base, value in enumerate(values):
            sums_ref[pl.ds(base, SLOTS, stride=16), :] = value
        for slot in range(SLOTS):
            place = place_of(row, slot)
            for base in range(9):
                lanes = slice(BLOCK * base, BLOCK * base + BLOCK)
                grad_ref[place, :, lanes] = (
                    grad_ref[place, :, lanes] + sums_ref[16 * slot + base : 16 * slot + base + 1, :]
                )

    groups = [list(range(first, first + GROUP)) for first in range(0, SLOTS, GROUP)]

    def both(row, bank):
        prepare(row, bank, True)
        for slot in range(SLOTS):
            exponents(slot, bank, True)
            glows(slot, 1 - bank)
        for group in groups:
            ahead(group, bank, True)
            back(group, 1 - bank)
        finish(jnp.maximum(row - 1, 0), 1 - bank)
        middle(row, bank)

    @pl.when(smooth)
    def _():
        def two(pair, _):
            both(2 * pair, 0)
            both(2 * pair + 1, 1)
            return 0

        lax.fori_loop(0, tiles // 2, two, 0)
        for slot in range(SLOTS):
            glows(slot, 1)
        for group in groups:
            back(group, 1)
        finish(tiles - 1, 1)

    @pl.when(jnp.logical_not(smooth))
    def _():
        def tile(row, _):
            def forth(slot, _):
                exponents(slot, 0, False)
                ahead([slot], 0, False)
                return 0

            def back_one(slot, _):
                glows(slot, 0)
                back([slot], 0)
                return 0

            prepare(row, 0, False)
            lax.fori_loop(0, SLOTS, forth, 0)
            middle(row, 0)
            lax.fori_loop(0, SLOTS, back_one, 0)
            finish(row, 0)
            return 0

        lax.fori_loop(0, tiles, tile, 0)


def blend(pairs, tile_place, arrived, target):
    quadratic, forms, moments = pixel_tables()
    tiles = target.shape[1]
    f32 = jnp.float32
    bf16 = jnp.bfloat16
    vmem = pl.BlockSpec(memory_space=pltpu.VMEM)
    smem = pl.BlockSpec(memory_space=pltpu.SMEM)
    return pl.pallas_call(
        blend_kernel,
        out_shape=(
            jax.ShapeDtypeStruct((3, tiles, PIXELS), f32),
            jax.ShapeDtypeStruct(arrived.shape, f32),
        ),
        in_specs=[smem, smem, vmem, vmem, vmem, vmem, vmem],
        out_specs=(vmem, vmem),
        scratch_shapes=[
            pltpu.VMEM((SLOTS * 16, BLOCK), f32),
            pltpu.VMEM((32 * SLOTS, BLOCK), f32),
            pltpu.VMEM((2, 16 * SLOTS, BLOCK), f32),
            pltpu.VMEM((2, 2, SLOTS, BLOCK), f32),
            pltpu.VMEM((BLOCK, 3 * PIXELS), f32),
            pltpu.VMEM((2, SLOTS, BLOCK, PIXELS), f32),
            pltpu.VMEM((2, SLOTS, BLOCK, PIXELS), f32),
            pltpu.VMEM((2, SLOTS, BLOCK, PIXELS), f32),
            pltpu.VMEM((2, SLOTS, BLOCK, PIXELS), f32),
            pltpu.VMEM((SLOTS, SEGMENTS, PIXELS), f32),
            pltpu.VMEM((SLOTS, 3 * SEGMENTS, PIXELS), f32),
            pltpu.VMEM((2, SLOTS, SEGMENTS, PIXELS), f32),
            pltpu.VMEM((2, SLOTS, SEGMENTS, PIXELS), f32),
            pltpu.VMEM((2, 16, PIXELS), f32),
            pltpu.VMEM((2, 32, PIXELS), f32),
            pltpu.VMEM((SLOTS * 16, BLOCK), f32),
        ],
        compiler_params=pltpu.CompilerParams(vmem_limit_bytes=24 << 20),
        cost_estimate=pl.CostEstimate(flops=200_000_000, bytes_accessed=6_000_000, transcendentals=4_000_000),
        name="blend",
    )(
        pairs, tile_place, arrived, target, jnp.asarray(quadratic, bf16),
        jnp.asarray(forms, bf16), jnp.asarray(moments, f32),
    )


def screen_of(raw, width, height):
    place_x, place_y, place_z = raw[0], raw[1], raw[2]
    screen_u = width * place_x / place_z + 0.5 * width
    screen_v = width * place_y / place_z + 0.5 * height
    inverse_one = jnp.exp(-2.0 * raw[3])
    inverse_two = jnp.exp(-2.0 * raw[4])
    cosine = jnp.cos(raw[5])
    sine = jnp.sin(raw[5])
    conic_a = cosine * cosine * inverse_one + sine * sine * inverse_two
    conic_b = cosine * sine * (inverse_one - inverse_two)
    conic_c = sine * sine * inverse_one + cosine * cosine * inverse_two
    log_opacity = jnp.minimum(raw[6], 0.0) - jnp.log1p(jnp.exp(-jnp.abs(raw[6])))
    length = jnp.sqrt(place_x * place_x + place_y * place_y + place_z * place_z)
    basis = harmonics(place_x / length, place_y / length, place_z / length)
    colors = []
    for channel in range(3):
        color = raw[7 + 16 * channel] * basis[0]
        for term in range(1, 16):
            color = color + raw[7 + 16 * channel + term] * basis[term]
        colors.append(0.5 + color)
    return [screen_u, screen_v, conic_a, conic_b, conic_c, log_opacity] + colors


def permuted(value, order):
    high, middle, low = (part.astype(jnp.bfloat16) for part in split3(value))
    rows = value.shape[0]
    found = jnp.dot(jnp.concatenate([high, middle, low], axis=0), order, preferred_element_type=jnp.float32)
    return found[0:rows] + found[rows : 2 * rows] + found[2 * rows : 3 * rows]


def project_kernel(width, height, splats_ref, order_ref, rows_ref):
    params, blocks, _ = splats_ref.shape
    raw = [splats_ref[base] for base in range(params)]
    found = screen_of(raw, width, height)
    conic_a, conic_b, conic_c = found[2:5]
    steep = conic_a > 1e-30
    over = lax.rsqrt(jnp.where(steep, conic_a, 1.0))
    form_xx = jnp.sqrt(conic_a)
    form_xy = jnp.where(steep, conic_b * over, 0.0)
    form_yy = jnp.where(steep, jnp.exp(-raw[3] - raw[4]) * over, jnp.sqrt(conic_c))
    rows = [found[0], found[1], FORM_SCALE * form_xx, FORM_SCALE * form_xy, FORM_SCALE * form_yy, LOG2_E * found[5]]
    for base, value in enumerate(rows + found[6:9]):
        value = permuted(value, order_ref[...])
        for block in range(blocks):
            rows_ref[block, :, BLOCK * base : BLOCK * base + BLOCK] = value[block : block + 1, :]


def project(splats, width, height):
    _, blocks, lanes = splats.shape
    vmem = pl.BlockSpec(memory_space=pltpu.VMEM)
    return pl.pallas_call(
        functools.partial(project_kernel, width, height),
        out_shape=jax.ShapeDtypeStruct((blocks, 1, 9 * lanes), jnp.float32),
        in_specs=[vmem, vmem],
        out_specs=vmem,
        cost_estimate=pl.CostEstimate(flops=5_000_000, bytes_accessed=1_000_000, transcendentals=30_000),
        compiler_params=pltpu.CompilerParams(vmem_limit_bytes=8 << 20),
        name="project",
    )(splats, jnp.asarray(lane_order(), jnp.bfloat16))


def asked_parts(held_ref, asked_ref, sem):
    share = held_ref.shape[0] // PARTS
    copies = []
    for part in range(PARTS):
        owners = pl.ds(part * share, share)
        copies.append(pltpu.make_async_copy(held_ref.at[owners], asked_ref.at[owners], sem.at[part]))
        copies[-1].start()
    return copies


def pack_kernel(held_ref, rows_ref, payload_ref, asked_ref, asked_sem):
    owners, _, most = asked_ref.shape
    share = owners // PARTS
    asked_copies = asked_parts(held_ref, asked_ref, asked_sem)
    for part in range(PARTS):
        asked_copies[part].wait()

        def one(step, _, first=part * share):
            owner = first + step
            for which in range(most):
                payload_ref[owner * most + which] = rows_ref[jnp.maximum(asked_ref[owner, 0, which], 0)]
            return 0

        lax.fori_loop(0, share, one, 0, unroll=8)


def pack(asked, rows):
    vmem = pl.BlockSpec(memory_space=pltpu.VMEM)
    return pl.pallas_call(
        pack_kernel,
        out_shape=jax.ShapeDtypeStruct((asked.shape[0] * asked.shape[2],) + rows.shape[1:], jnp.float32),
        in_specs=[vmem, vmem],
        out_specs=vmem,
        scratch_shapes=[pltpu.SMEM(asked.shape, jnp.int32), pltpu.SemaphoreType.DMA((PARTS,))],
        cost_estimate=pl.CostEstimate(flops=0, bytes_accessed=2_000_000, transcendentals=0),
        compiler_params=pltpu.CompilerParams(vmem_limit_bytes=8 << 20),
        name="pack",
    )(asked, rows)


def update_kernel(
    width, height, held_ref, returned_ref, splats_ref, one_ref, two_ref, order_ref,
    grad_out_ref, step_out_ref, asked_ref, asked_sem, grad_ref, step_ref, sem, sum_ref, rows_ref,
    pulled_ref, *lane_refs,
):
    params, blocks, _ = splats_ref.shape
    asked_copies = asked_parts(held_ref, asked_ref, asked_sem)
    for lane_ref in lane_refs:
        lane_ref[...] = jnp.zeros_like(lane_ref)

    owners, _, most = asked_ref.shape
    step = len(lane_refs) // most

    def gather(group, _):
        for lane, lane_ref in enumerate(lane_refs):
            block = jnp.maximum(asked_ref[group * step + lane // most, 0, lane % most], 0)
            lane_ref[block] = lane_ref[block] + returned_ref[group * len(lane_refs) + lane]
        return 0

    share = owners // step // PARTS
    for part in range(PARTS):
        asked_copies[part].wait()
        lax.fori_loop(part * share, part * share + share, gather, 0, unroll=2)
    for block in range(blocks):
        value = lane_refs[0][block]
        for lane_ref in lane_refs[1:]:
            value = value + lane_ref[block]
        sum_ref[block] = value
        for base in range(9):
            rows_ref[blocks * base + block : blocks * base + block + 1, :] = sum_ref[
                block, :, BLOCK * base : BLOCK * base + BLOCK
            ]
    pulled_ref[...] = permuted(rows_ref[...], order_ref[...])
    copies = []
    for first in range(0, blocks, 8):
        eight = slice(first, first + 8)
        raw = [splats_ref[base, eight, :] for base in range(params)]
        summed = [pulled_ref[blocks * base + first : blocks * base + first + 8, :] for base in range(9)]
        found, pull = jax.vjp(functools.partial(screen_of, width=width, height=height), raw)
        conic_a, conic_b, conic_c = found[2:5]
        (pulled,) = pull(
            [
                conic_a * summed[0] + conic_b * summed[1],
                conic_b * summed[0] + conic_c * summed[1],
                -0.5 * summed[2],
                -summed[3],
                -0.5 * summed[4],
                summed[5],
            ]
            + summed[6:9]
        )
        for base, grad in enumerate(pulled):
            grad_ref[base, eight, :] = grad
            moved = 0.9 * one_ref[base, eight, :] + 0.1 * grad
            second = 0.999 * two_ref[base, eight, :] + 0.001 * grad * grad
            step_ref[base, eight, :] = moved / (jnp.sqrt(second) + 1e-08)
        for which, (held, out) in enumerate(((grad_ref, grad_out_ref), (step_ref, step_out_ref))):
            copies.append(
                pltpu.make_async_copy(
                    held.at[:, pl.ds(first, 8), :], out.at[:, pl.ds(first, 8), :], sem.at[first // 8, which]
                )
            )
            copies[-1].start()
    for copy in copies:
        copy.wait()


def update(asked, returned, splats, moment_one, moment_two, width, height):
    params, blocks, lanes = splats.shape
    vmem = pl.BlockSpec(memory_space=pltpu.VMEM)
    f32 = jnp.float32
    shape = jax.ShapeDtypeStruct(splats.shape, f32)
    row_sums = pltpu.VMEM((blocks, 1, 9 * lanes), f32)
    return pl.pallas_call(
        functools.partial(update_kernel, width, height),
        out_shape=(shape, shape),
        in_specs=[vmem] * 6,
        out_specs=(pl.BlockSpec(memory_space=pl.ANY), pl.BlockSpec(memory_space=pl.ANY)),
        scratch_shapes=[
            pltpu.SMEM(asked.shape, jnp.int32),
            pltpu.SemaphoreType.DMA((PARTS,)),
            pltpu.VMEM(splats.shape, f32),
            pltpu.VMEM(splats.shape, f32),
            pltpu.SemaphoreType.DMA((blocks // 8, 2)),
            row_sums,
            pltpu.VMEM((9 * blocks, lanes), f32),
            pltpu.VMEM((9 * blocks, lanes), f32),
        ]
        + [row_sums] * 8,
        cost_estimate=pl.CostEstimate(flops=8_000_000, bytes_accessed=6_000_000, transcendentals=500_000),
        compiler_params=pltpu.CompilerParams(vmem_limit_bytes=16 << 20),
        name="update",
    )(asked, returned, splats, moment_one, moment_two, jnp.asarray(lane_order().T, jnp.bfloat16))


def trade(payload):
    return lax.all_to_all(payload, ("gx", "gy"), split_axis=0, concat_axis=0, tiled=True)


def local(splats, moment_one, moment_two, target, tile_place, pairs, fetch):
    devices = lax.axis_size("gx") * lax.axis_size("gy")
    tiles_here = target.shape[0]
    width = 16.0 * TX
    height = 16.0 * (tiles_here * devices // TX)
    flat, first_moment, second_moment = (
        jnp.transpose(value, (1, 0, 2)) for value in (splats, moment_one, moment_two)
    )
    asked = trade(fetch.reshape(fetch.shape[1], 1, fetch.shape[2]))
    rows = project(flat, width, height)
    arrived = trade(pack(asked, rows))
    image, received = blend(jnp.transpose(pairs), tile_place, arrived, jnp.transpose(target, (1, 0, 2)))
    grad, step = update(asked, trade(received), flat, first_moment, second_moment, width, height)
    return tuple(jnp.transpose(value, (1, 0, 2)) for value in (image, grad, step))


def solution(mesh):
    return jax.shard_map(
        local,
        mesh=mesh,
        in_specs=(
            P(("gx", "gy"), None, None),
            P(("gx", "gy"), None, None),
            P(("gx", "gy"), None, None),
            P(("gx", "gy"), None, None),
            P(("gx", "gy")),
            P(("gx", "gy"), None),
            P(("gx", "gy"), None, None),
        ),
        out_specs=(
            P(("gx", "gy"), None, None),
            P(("gx", "gy"), None, None),
            P(("gx", "gy"), None, None),
        ),
        check_vma=False,
    )
```

```python
import functools

import jax
import jax.numpy as jnp
import numpy as np
from jax import lax
from jax.experimental import pallas as pl
from jax.experimental.pallas import tpu as pltpu
from jax.sharding import PartitionSpec as P

TX = 16
BLOCK = 128
SEGMENTS = 8
STEPS = BLOCK // SEGMENTS
SLOTS = 8
PIXELS = 256
LOG2_E = 1.4426950408889634
FORM_SCALE = 0.8493218002880191
SMOOTH_TRACE = 0.75
GROUP = 2
PARTS = 4

HARMONIC_ZERO = 0.28209479177387814
HARMONIC_ONE = 0.4886025119029199
HARMONIC_TWO = (
    1.0925484305920792,
    -1.0925484305920792,
    0.31539156525252005,
    -1.0925484305920792,
    0.5462742152960396,
)
HARMONIC_THREE = (
    -0.5900435899266435,
    2.890611442640554,
    -0.4570457994644658,
    0.3731763325901154,
    -0.4570457994644658,
    1.445305721320277,
    -0.5900435899266435,
)


def harmonics(east, north, ahead):
    east_east = east * east
    north_north = north * north
    ahead_ahead = ahead * ahead
    terms = [
        jnp.full_like(east, HARMONIC_ZERO),
        -HARMONIC_ONE * north,
        HARMONIC_ONE * ahead,
        -HARMONIC_ONE * east,
        HARMONIC_TWO[0] * east * north,
        HARMONIC_TWO[1] * north * ahead,
        HARMONIC_TWO[2] * (2.0 * ahead_ahead - east_east - north_north),
        HARMONIC_TWO[3] * east * ahead,
        HARMONIC_TWO[4] * (east_east - north_north),
        HARMONIC_THREE[0] * north * (3.0 * east_east - north_north),
        HARMONIC_THREE[1] * east * north * ahead,
        HARMONIC_THREE[2] * north * (4.0 * ahead_ahead - east_east - north_north),
        HARMONIC_THREE[3] * ahead * (2.0 * ahead_ahead - 3.0 * east_east - 3.0 * north_north),
        HARMONIC_THREE[4] * east * (4.0 * ahead_ahead - east_east - north_north),
        HARMONIC_THREE[5] * ahead * (east_east - north_north),
        HARMONIC_THREE[6] * east * (east_east - 3.0 * north_north),
    ]
    return terms


def lane_order(back):
    splat = lax.broadcasted_iota(jnp.int32, (BLOCK, BLOCK), 1 if back else 0)
    lane = lax.broadcasted_iota(jnp.int32, (BLOCK, BLOCK), 0 if back else 1)
    held = STEPS * lax.rem(lane, SEGMENTS) + lax.div(lane, SEGMENTS)
    return (splat == held).astype(jnp.float32).astype(jnp.bfloat16)


def pixel_tables():
    pixel = np.arange(PIXELS)
    across = (pixel % 16) - 7.5
    down = (pixel // 16) - 7.5
    ones = np.ones(PIXELS)
    moments = np.zeros((8, PIXELS), np.float32)
    moments[0:6] = [ones, across, down, across * across, across * down, down * down]
    quadratic = np.zeros((32, PIXELS), np.float32)
    for base in range(6):
        quadratic[3 * base : 3 * base + 3] = moments[base]
    forms = np.zeros((32, 3 * PIXELS), np.float32)
    forms[0:3, :PIXELS] = across
    forms[3:6, :PIXELS] = down
    forms[6:9, :PIXELS] = ones
    forms[9:12, PIXELS : 2 * PIXELS] = down
    forms[12:15, PIXELS : 2 * PIXELS] = ones
    forms[15:18, 2 * PIXELS :] = ones
    return quadratic, forms, moments


def rounded(value):
    return value.astype(jnp.bfloat16).astype(jnp.float32)


def split3(value):
    high = rounded(value)
    rest = value - high
    middle = rounded(rest)
    return high, middle, rest - middle


def split2(value):
    high = rounded(value)
    return high, rounded(value - high)


CONTRACT_ROWS = (((0,), (0,)), ((), ()))
CONTRACT_LANES = (((1,), (1,)), ((), ()))


def blend_kernel(
    pairs_ref, place_ref, arrived_ref, target_ref, quadratic_ref, forms_ref, moments_ref,
    image_ref, grad_ref,
    block_ref, form_ref, tint_ref, center_ref, steep_ref, power_ref, glow_power_ref,
    alpha_ref, weight_ref, trans_ref, local_ref, carry_ref, behind_ref, glow_ref, rows_ref,
    sums_ref,
):
    f32 = jnp.float32
    bf16 = jnp.bfloat16
    tiles = target_ref.shape[1]
    segment = lax.broadcasted_iota(jnp.int32, (SEGMENTS, PIXELS), 0)
    slot_row = lax.broadcasted_iota(jnp.int32, (SLOTS, BLOCK), 0)
    lane_segment = lax.rem(lax.broadcasted_iota(jnp.int32, (SEGMENTS, BLOCK), 1), SEGMENTS)
    own_segment = (lane_segment == lax.broadcasted_iota(jnp.int32, (SEGMENTS, BLOCK), 0)).astype(f32)

    def clear(place, steep):
        grad_ref[place] = jnp.zeros(grad_ref.shape[1:], f32)
        forms = arrived_ref[place, :, 2 * BLOCK : 5 * BLOCK]
        return jnp.maximum(steep, forms * forms)

    steep = lax.fori_loop(0, grad_ref.shape[0], clear, jnp.zeros((1, 3 * BLOCK), f32), unroll=8)
    smooth = (
        jnp.max(steep[:, 0:BLOCK] + steep[:, BLOCK : 2 * BLOCK] + steep[:, 2 * BLOCK : 3 * BLOCK])
        <= SMOOTH_TRACE
    )
    form_ref[...] = jnp.zeros_like(form_ref)
    for empty in (tint_ref, center_ref, rows_ref, glow_ref, carry_ref, behind_ref):
        empty[...] = jnp.zeros_like(empty)
    for bank in range(2):
        rows_ref[bank, 0:8, :] = moments_ref[...]

    def clear_steps(slot, _):
        alpha_ref[1, slot] = jnp.zeros(alpha_ref.shape[2:], f32)
        weight_ref[1, slot] = jnp.zeros(weight_ref.shape[2:], f32)
        return 0

    lax.fori_loop(0, SLOTS, clear_steps, 0)

    def place_of(row, slot):
        return jnp.maximum(pairs_ref[slot, row], 0)

    def prepare(row, bank, quick):
        view = place_ref[row]
        center_x = (16 * lax.rem(view, TX) + 8).astype(f32)
        center_y = (16 * lax.div(view, TX) + 8).astype(f32)
        live = jnp.zeros((SLOTS, BLOCK), f32)
        for slot in range(SLOTS):
            live = jnp.where(slot_row == slot, (pairs_ref[slot, row] >= 0).astype(f32), live)
            place = place_of(row, slot)
            for base in range(9):
                block_ref[16 * slot + base : 16 * slot + base + 1, :] = arrived_ref[
                    place, :, BLOCK * base : BLOCK * base + BLOCK
                ]

        def fetched(base):
            return block_ref[pl.ds(base, SLOTS, stride=16), :]

        across = fetched(0) - center_x
        down = fetched(1) - center_y
        center_ref[bank, 0] = across
        center_ref[bank, 1] = down
        form_xx, form_xy, form_yy = fetched(2), fetched(3), fetched(4)
        log_opacity = jnp.where(live > 0.0, fetched(5), -1e9)
        shift_one = -(form_xx * across + form_xy * down)
        shift_two = -(form_yy * down)
        if quick:
            shift_one = jnp.clip(shift_one, -1e4, 1e4)
            shift_two = jnp.clip(shift_two, -1e4, 1e4)
            values = (
                log_opacity - shift_one * shift_one - shift_two * shift_two,
                -2.0 * (form_xx * shift_one),
                -2.0 * (form_xy * shift_one + form_yy * shift_two),
                -(form_xx * form_xx),
                -2.0 * (form_xx * form_xy),
                -(form_xy * form_xy + form_yy * form_yy),
            )
        else:
            values = (form_xx, form_xy, shift_one, form_yy, shift_two, log_opacity)
        for base, value in enumerate(values):
            for part, piece in enumerate(split3(value)):
                form_ref[pl.ds(8 * (3 * base + part), SLOTS), :] = piece
        for channel in range(3):
            high, low = split2(fetched(6 + channel))
            for base, piece in enumerate((high, low, high)):
                tint_ref[bank, pl.ds(8 * (3 * base + channel), SLOTS), :] = piece

    def exponents(slot, bank, quick):
        lhs = form_ref[pl.ds(slot, 32, stride=8), :].astype(bf16)
        if quick:
            power_ref[bank, slot] = lax.dot_general(
                lhs, quadratic_ref[...], CONTRACT_ROWS, preferred_element_type=f32
            )
            return
        steep_ref[...] = lax.dot_general(lhs, forms_ref[...], CONTRACT_ROWS, preferred_element_type=f32)

    def joined(kept, inner):
        halves = [jnp.concatenate([piece for part in kept[2 * inner + half] for piece in part], axis=0) for half in range(2)]
        return jnp.concatenate(halves, axis=1)

    def ahead(slots, bank, quick):
        chains = [(inner, half) for inner in range(len(slots)) for half in range(2)]
        trans = [jnp.ones((SEGMENTS, 128), f32) for _ in chains]
        kept = [[[None] * (STEPS // 2) for _ in range(2)] for _ in chains]

        def keep(chain, pair, value):
            high = value.astype(bf16)
            kept[chain][0][pair] = high
            kept[chain][1][pair] = (value - high.astype(f32)).astype(bf16)

        for pair in range(STEPS // 2):
            weights = [[] for _ in chains]
            for step in (2 * pair, 2 * pair + 1):
                eight = slice(8 * step, 8 * step + 8)
                for chain, (inner, half) in enumerate(chains):
                    lanes = slice(128 * half, 128 * half + 128)
                    if quick:
                        exponent = jnp.minimum(power_ref[bank, slots[inner], eight, lanes], 0.0)
                    else:
                        one = steep_ref[eight, lanes]
                        two = steep_ref[eight, 256 + 128 * half : 384 + 128 * half]
                        three = steep_ref[eight, 512 + 128 * half : 640 + 128 * half]
                        exponent = three - one * one - two * two
                    alpha = jnp.exp2(exponent)
                    weight = alpha * trans[chain]
                    trans[chain] = trans[chain] - weight
                    alpha_ref[bank, slots[inner], eight, lanes] = alpha
                    weight_ref[bank, slots[inner], eight, lanes] = weight
                    weights[chain].append(weight)
            for chain in range(len(chains)):
                keep(chain, pair, jnp.concatenate(weights[chain], axis=0))
        for chain, (inner, half) in enumerate(chains):
            trans_ref[slots[inner], :, 128 * half : 128 * half + 128] = trans[chain]
        for inner, slot in enumerate(slots):
            parts = [own_segment * tint_ref[bank, pl.ds(8 * base + slot, 1), :] for base in range(6)]
            lhs = jnp.concatenate(parts, axis=0).astype(bf16)
            found = lax.dot_general(
                jnp.concatenate([lhs, lhs], axis=1), joined(kept, inner),
                (((1,), (0,)), ((), ())), preferred_element_type=f32,
            )
            local_ref[slot] = found[0:24] + found[24:48]

    def middle(row, bank):
        before = jnp.ones((1, PIXELS), f32)
        seen = [jnp.zeros((SEGMENTS, PIXELS), f32) for _ in range(3)]
        for slot in range(SLOTS):
            through = trans_ref[slot]
            for reach in (1, 2, 4):
                through = through * jnp.where(segment >= reach, pltpu.roll(through, reach, 0), 1.0)
            carry = jnp.where(segment >= 1, pltpu.roll(through, 1, 0), 1.0) * before
            carry_ref[bank, slot] = carry
            for channel in range(3):
                seen[channel] = seen[channel] + carry * local_ref[slot, 8 * channel : 8 * channel + 8, :]
            before = before * through[7:8]
        glow = []
        for channel in range(3):
            color = jnp.sum(seen[channel], axis=0, keepdims=True)
            image_ref[channel, pl.ds(row, 1), :] = color
            value = (color - target_ref[channel, pl.ds(row, 1), :]) * (2.0 / 512.0)
            glow.append(value)
            high, low = split2(value)
            for base, piece in enumerate((high, high, low)):
                glow_ref[bank, 3 * base + channel : 3 * base + channel + 1, :] = piece
            rows_ref[bank, 8 + channel : 9 + channel, :] = high
            rows_ref[bank, 16 + channel : 17 + channel, :] = low

        after = jnp.zeros((1, PIXELS), f32)
        for slot in reversed(range(SLOTS)):
            through = trans_ref[slot]
            light = (
                local_ref[slot, 0:8, :] * glow[0]
                + local_ref[slot, 8:16, :] * glow[1]
                + local_ref[slot, 16:24, :] * glow[2]
            )
            for reach in (1, 2, 4):
                inside = segment < SEGMENTS - reach
                light = light + through * jnp.where(inside, pltpu.roll(light, SEGMENTS - reach, 0), 0.0)
                through = through * jnp.where(inside, pltpu.roll(through, SEGMENTS - reach, 0), 1.0)
            start = light + through * after
            behind_ref[bank, slot] = jnp.where(segment < SEGMENTS - 1, pltpu.roll(start, SEGMENTS - 1, 0), after)
            after = start[0:1]

    def glows(slot, bank):
        glow_power_ref[bank, slot] = lax.dot_general(
            tint_ref[bank, pl.ds(slot, 16, stride=8), :].astype(bf16), glow_ref[bank].astype(bf16),
            CONTRACT_ROWS, preferred_element_type=f32,
        )

    def back(slots, bank):
        chains = [(inner, half) for inner in range(len(slots)) for half in range(2)]
        behind = [behind_ref[bank, slots[inner], :, 128 * half : 128 * half + 128] for inner, half in chains]
        kept = [[[None] * (STEPS // 2) for _ in range(4)] for _ in chains]
        for pair in reversed(range(STEPS // 2)):
            pulls = [[] for _ in chains]
            weights = [[] for _ in chains]
            for step in (2 * pair + 1, 2 * pair):
                eight = slice(8 * step, 8 * step + 8)
                for chain, (inner, half) in enumerate(chains):
                    lanes = slice(128 * half, 128 * half + 128)
                    alpha = alpha_ref[bank, slots[inner], eight, lanes]
                    carry = carry_ref[bank, slots[inner], :, lanes]
                    weight = weight_ref[bank, slots[inner], eight, lanes] * carry
                    gain = glow_power_ref[bank, slots[inner], eight, lanes] - behind[chain]
                    behind[chain] = behind[chain] + alpha * gain
                    pulls[chain].append(weight * gain)
                    weights[chain].append(weight)
            for chain in range(len(chains)):
                for base, parts in ((0, pulls[chain]), (2, weights[chain])):
                    value = jnp.concatenate([parts[1], parts[0]], axis=0)
                    high = value.astype(bf16)
                    kept[chain][base][pair] = high
                    kept[chain][base + 1][pair] = (value - high.astype(f32)).astype(bf16)
        lhs_rows = rows_ref[bank].astype(bf16)
        for inner, slot in enumerate(slots):
            found = lax.dot_general(
                lhs_rows, joined(kept, inner), CONTRACT_LANES, preferred_element_type=f32
            )
            tints = found[8:24, 256:384] + found[8:24, 384:512]
            sums_ref[pl.ds(16 * slot, 8), :] = found[0:8, 0:128] + found[0:8, 128:256]
            sums_ref[pl.ds(16 * slot + 8, 8), :] = tints[0:8] + tints[8:16]

    def finish(row, bank):
        across = center_ref[bank, 0]
        down = center_ref[bank, 1]

        def summed(base):
            return sums_ref[pl.ds(base, SLOTS, stride=16), :]

        total, sum_x, sum_y = summed(0), summed(1), summed(2)
        off_x = sum_x - across * total
        off_y = sum_y - down * total
        sum_xx = summed(3) - across * (sum_x + off_x)
        sum_xy = summed(4) - across * sum_y - down * off_x
        sum_yy = summed(5) - down * (sum_y + off_y)
        values = (off_x, off_y, sum_xx, sum_xy, sum_yy, total, summed(8), summed(9), summed(10))
        for base, value in enumerate(values):
            sums_ref[pl.ds(base, SLOTS, stride=16), :] = value
        for slot in range(SLOTS):
            place = place_of(row, slot)
            for base in range(9):
                lanes = slice(BLOCK * base, BLOCK * base + BLOCK)
                grad_ref[place, :, lanes] = (
                    grad_ref[place, :, lanes] + sums_ref[16 * slot + base : 16 * slot + base + 1, :]
                )

    groups = [list(range(first, first + GROUP)) for first in range(0, SLOTS, GROUP)]

    def both(row, bank):
        prepare(row, bank, True)
        for slot in range(SLOTS):
            exponents(slot, bank, True)
            glows(slot, 1 - bank)
        for group in groups:
            ahead(group, bank, True)
            back(group, 1 - bank)
        finish(jnp.maximum(row - 1, 0), 1 - bank)
        middle(row, bank)

    @pl.when(smooth)
    def _():
        def two(pair, _):
            both(2 * pair, 0)
            both(2 * pair + 1, 1)
            return 0

        lax.fori_loop(0, tiles // 2, two, 0)
        for slot in range(SLOTS):
            glows(slot, 1)
        for group in groups:
            back(group, 1)
        finish(tiles - 1, 1)

    @pl.when(jnp.logical_not(smooth))
    def _():
        def tile(row, _):
            def forth(slot, _):
                exponents(slot, 0, False)
                ahead([slot], 0, False)
                return 0

            def back_one(slot, _):
                glows(slot, 0)
                back([slot], 0)
                return 0

            prepare(row, 0, False)
            lax.fori_loop(0, SLOTS, forth, 0)
            middle(row, 0)
            lax.fori_loop(0, SLOTS, back_one, 0)
            finish(row, 0)
            return 0

        lax.fori_loop(0, tiles, tile, 0)


def blend(pairs, tile_place, arrived, target):
    quadratic, forms, moments = pixel_tables()
    tiles = target.shape[1]
    f32 = jnp.float32
    bf16 = jnp.bfloat16
    vmem = pl.BlockSpec(memory_space=pltpu.VMEM)
    smem = pl.BlockSpec(memory_space=pltpu.SMEM)
    return pl.pallas_call(
        blend_kernel,
        out_shape=(
            jax.ShapeDtypeStruct((3, tiles, PIXELS), f32),
            jax.ShapeDtypeStruct(arrived.shape, f32),
        ),
        in_specs=[smem, smem, vmem, vmem, vmem, vmem, vmem],
        out_specs=(vmem, vmem),
        scratch_shapes=[
            pltpu.VMEM((SLOTS * 16, BLOCK), f32),
            pltpu.VMEM((32 * SLOTS, BLOCK), f32),
            pltpu.VMEM((2, 16 * SLOTS, BLOCK), f32),
            pltpu.VMEM((2, 2, SLOTS, BLOCK), f32),
            pltpu.VMEM((BLOCK, 3 * PIXELS), f32),
            pltpu.VMEM((2, SLOTS, BLOCK, PIXELS), f32),
            pltpu.VMEM((2, SLOTS, BLOCK, PIXELS), f32),
            pltpu.VMEM((2, SLOTS, BLOCK, PIXELS), f32),
            pltpu.VMEM((2, SLOTS, BLOCK, PIXELS), f32),
            pltpu.VMEM((SLOTS, SEGMENTS, PIXELS), f32),
            pltpu.VMEM((SLOTS, 3 * SEGMENTS, PIXELS), f32),
            pltpu.VMEM((2, SLOTS, SEGMENTS, PIXELS), f32),
            pltpu.VMEM((2, SLOTS, SEGMENTS, PIXELS), f32),
            pltpu.VMEM((2, 16, PIXELS), f32),
            pltpu.VMEM((2, 32, PIXELS), f32),
            pltpu.VMEM((SLOTS * 16, BLOCK), f32),
        ],
        compiler_params=pltpu.CompilerParams(vmem_limit_bytes=24 << 20),
        cost_estimate=pl.CostEstimate(flops=200_000_000, bytes_accessed=6_000_000, transcendentals=4_000_000),
        name="blend",
    )(
        pairs, tile_place, arrived, target, jnp.asarray(quadratic, bf16),
        jnp.asarray(forms, bf16), jnp.asarray(moments, f32),
    )


def screen_of(raw, width, height):
    place_x, place_y, place_z = raw[0], raw[1], raw[2]
    screen_u = width * place_x / place_z + 0.5 * width
    screen_v = width * place_y / place_z + 0.5 * height
    inverse_one = jnp.exp(-2.0 * raw[3])
    inverse_two = jnp.exp(-2.0 * raw[4])
    cosine = jnp.cos(raw[5])
    sine = jnp.sin(raw[5])
    conic_a = cosine * cosine * inverse_one + sine * sine * inverse_two
    conic_b = cosine * sine * (inverse_one - inverse_two)
    conic_c = sine * sine * inverse_one + cosine * cosine * inverse_two
    log_opacity = jnp.minimum(raw[6], 0.0) - jnp.log1p(jnp.exp(-jnp.abs(raw[6])))
    length = jnp.sqrt(place_x * place_x + place_y * place_y + place_z * place_z)
    basis = harmonics(place_x / length, place_y / length, place_z / length)
    colors = []
    for channel in range(3):
        color = raw[7 + 16 * channel] * basis[0]
        for term in range(1, 16):
            color = color + raw[7 + 16 * channel + term] * basis[term]
        colors.append(0.5 + color)
    return [screen_u, screen_v, conic_a, conic_b, conic_c, log_opacity] + colors


def permuted(value, order):
    high, middle, low = (part.astype(jnp.bfloat16) for part in split3(value))
    rows = value.shape[0]
    found = jnp.dot(jnp.concatenate([high, middle, low], axis=0), order, preferred_element_type=jnp.float32)
    return found[0:rows] + found[rows : 2 * rows] + found[2 * rows : 3 * rows]


def project_kernel(width, height, splats_ref, rows_ref):
    params, blocks, _ = splats_ref.shape
    raw = [splats_ref[base] for base in range(params)]
    found = screen_of(raw, width, height)
    conic_a, conic_b, conic_c = found[2:5]
    steep = conic_a > 1e-30
    over = lax.rsqrt(jnp.where(steep, conic_a, 1.0))
    form_xx = jnp.sqrt(conic_a)
    form_xy = jnp.where(steep, conic_b * over, 0.0)
    form_yy = jnp.where(steep, jnp.exp(-raw[3] - raw[4]) * over, jnp.sqrt(conic_c))
    rows = [found[0], found[1], FORM_SCALE * form_xx, FORM_SCALE * form_xy, FORM_SCALE * form_yy, LOG2_E * found[5]]
    order = lane_order(False)
    for base, value in enumerate(rows + found[6:9]):
        value = permuted(value, order)
        for block in range(blocks):
            rows_ref[block, :, BLOCK * base : BLOCK * base + BLOCK] = value[block : block + 1, :]


def project(splats, width, height):
    _, blocks, lanes = splats.shape
    vmem = pl.BlockSpec(memory_space=pltpu.VMEM)
    return pl.pallas_call(
        functools.partial(project_kernel, width, height),
        out_shape=jax.ShapeDtypeStruct((blocks, 1, 9 * lanes), jnp.float32),
        in_specs=[vmem],
        out_specs=vmem,
        cost_estimate=pl.CostEstimate(flops=5_000_000, bytes_accessed=1_000_000, transcendentals=30_000),
        compiler_params=pltpu.CompilerParams(vmem_limit_bytes=8 << 20),
        name="project",
    )(splats)


def asked_parts(held_ref, asked_ref, sem):
    share = held_ref.shape[0] // PARTS
    copies = []
    for part in range(PARTS):
        owners = pl.ds(part * share, share)
        copies.append(pltpu.make_async_copy(held_ref.at[owners], asked_ref.at[owners], sem.at[part]))
        copies[-1].start()
    return copies


def pack_kernel(held_ref, rows_ref, payload_ref, asked_ref, asked_sem):
    owners, _, most = asked_ref.shape
    share = owners // PARTS
    asked_copies = asked_parts(held_ref, asked_ref, asked_sem)
    for part in range(PARTS):
        asked_copies[part].wait()

        def one(step, _, first=part * share):
            owner = first + step
            for which in range(most):
                payload_ref[owner * most + which] = rows_ref[jnp.maximum(asked_ref[owner, 0, which], 0)]
            return 0

        lax.fori_loop(0, share, one, 0, unroll=8)


def pack(asked, rows):
    vmem = pl.BlockSpec(memory_space=pltpu.VMEM)
    return pl.pallas_call(
        pack_kernel,
        out_shape=jax.ShapeDtypeStruct((asked.shape[0] * asked.shape[2],) + rows.shape[1:], jnp.float32),
        in_specs=[vmem, vmem],
        out_specs=vmem,
        scratch_shapes=[pltpu.SMEM(asked.shape, jnp.int32), pltpu.SemaphoreType.DMA((PARTS,))],
        cost_estimate=pl.CostEstimate(flops=0, bytes_accessed=2_000_000, transcendentals=0),
        compiler_params=pltpu.CompilerParams(vmem_limit_bytes=8 << 20),
        name="pack",
    )(asked, rows)


def update_kernel(
    width, height, held_ref, returned_ref, splats_ref, one_ref, two_ref,
    grad_out_ref, step_out_ref, asked_ref, asked_sem, grad_ref, step_ref, sem, sum_ref, rows_ref,
    pulled_ref, *lane_refs,
):
    params, blocks, _ = splats_ref.shape
    asked_copies = asked_parts(held_ref, asked_ref, asked_sem)
    for lane_ref in lane_refs:
        lane_ref[...] = jnp.zeros_like(lane_ref)

    owners, _, most = asked_ref.shape
    step = len(lane_refs) // most

    def gather(group, _):
        for lane, lane_ref in enumerate(lane_refs):
            block = jnp.maximum(asked_ref[group * step + lane // most, 0, lane % most], 0)
            lane_ref[block] = lane_ref[block] + returned_ref[group * len(lane_refs) + lane]
        return 0

    share = owners // step // PARTS
    for part in range(PARTS):
        asked_copies[part].wait()
        lax.fori_loop(part * share, part * share + share, gather, 0, unroll=2)
    for block in range(blocks):
        value = lane_refs[0][block]
        for lane_ref in lane_refs[1:]:
            value = value + lane_ref[block]
        sum_ref[block] = value
        for base in range(9):
            rows_ref[blocks * base + block : blocks * base + block + 1, :] = sum_ref[
                block, :, BLOCK * base : BLOCK * base + BLOCK
            ]
    pulled_ref[...] = permuted(rows_ref[...], lane_order(True))
    copies = []
    for first in range(0, blocks, 8):
        eight = slice(first, first + 8)
        raw = [splats_ref[base, eight, :] for base in range(params)]
        summed = [pulled_ref[blocks * base + first : blocks * base + first + 8, :] for base in range(9)]
        found, pull = jax.vjp(functools.partial(screen_of, width=width, height=height), raw)
        conic_a, conic_b, conic_c = found[2:5]
        (pulled,) = pull(
            [
                conic_a * summed[0] + conic_b * summed[1],
                conic_b * summed[0] + conic_c * summed[1],
                -0.5 * summed[2],
                -summed[3],
                -0.5 * summed[4],
                summed[5],
            ]
            + summed[6:9]
        )
        for base, grad in enumerate(pulled):
            grad_ref[base, eight, :] = grad
            moved = 0.9 * one_ref[base, eight, :] + 0.1 * grad
            second = 0.999 * two_ref[base, eight, :] + 0.001 * grad * grad
            step_ref[base, eight, :] = moved / (jnp.sqrt(second) + 1e-08)
        for which, (held, out) in enumerate(((grad_ref, grad_out_ref), (step_ref, step_out_ref))):
            copies.append(
                pltpu.make_async_copy(
                    held.at[:, pl.ds(first, 8), :], out.at[:, pl.ds(first, 8), :], sem.at[first // 8, which]
                )
            )
            copies[-1].start()
    for copy in copies:
        copy.wait()


def update(asked, returned, splats, moment_one, moment_two, width, height):
    params, blocks, lanes = splats.shape
    vmem = pl.BlockSpec(memory_space=pltpu.VMEM)
    f32 = jnp.float32
    shape = jax.ShapeDtypeStruct(splats.shape, f32)
    row_sums = pltpu.VMEM((blocks, 1, 9 * lanes), f32)
    return pl.pallas_call(
        functools.partial(update_kernel, width, height),
        out_shape=(shape, shape),
        in_specs=[vmem] * 5,
        out_specs=(pl.BlockSpec(memory_space=pl.ANY), pl.BlockSpec(memory_space=pl.ANY)),
        scratch_shapes=[
            pltpu.SMEM(asked.shape, jnp.int32),
            pltpu.SemaphoreType.DMA((PARTS,)),
            pltpu.VMEM(splats.shape, f32),
            pltpu.VMEM(splats.shape, f32),
            pltpu.SemaphoreType.DMA((blocks // 8, 2)),
            row_sums,
            pltpu.VMEM((9 * blocks, lanes), f32),
            pltpu.VMEM((9 * blocks, lanes), f32),
        ]
        + [row_sums] * 8,
        cost_estimate=pl.CostEstimate(flops=8_000_000, bytes_accessed=6_000_000, transcendentals=500_000),
        compiler_params=pltpu.CompilerParams(vmem_limit_bytes=16 << 20),
        name="update",
    )(asked, returned, splats, moment_one, moment_two)


def trade(payload):
    return lax.all_to_all(payload, ("gx", "gy"), split_axis=0, concat_axis=0, tiled=True)


def local(splats, moment_one, moment_two, target, tile_place, pairs, fetch):
    devices = lax.axis_size("gx") * lax.axis_size("gy")
    tiles_here = target.shape[0]
    width = 16.0 * TX
    height = 16.0 * (tiles_here * devices // TX)
    flat, first_moment, second_moment = (
        jnp.transpose(value, (1, 0, 2)) for value in (splats, moment_one, moment_two)
    )
    asked = trade(fetch.reshape(fetch.shape[1], 1, fetch.shape[2]))
    rows = project(flat, width, height)
    arrived = trade(pack(asked, rows))
    image, received = blend(jnp.transpose(pairs), tile_place, arrived, jnp.transpose(target, (1, 0, 2)))
    grad, step = update(asked, trade(received), flat, first_moment, second_moment, width, height)
    return tuple(jnp.transpose(value, (1, 0, 2)) for value in (image, grad, step))


def solution(mesh):
    return jax.shard_map(
        local,
        mesh=mesh,
        in_specs=(
            P(("gx", "gy"), None, None),
            P(("gx", "gy"), None, None),
            P(("gx", "gy"), None, None),
            P(("gx", "gy"), None, None),
            P(("gx", "gy")),
            P(("gx", "gy"), None),
            P(("gx", "gy"), None, None),
        ),
        out_specs=(
            P(("gx", "gy"), None, None),
            P(("gx", "gy"), None, None),
            P(("gx", "gy"), None, None),
        ),
        check_vma=False,
    )
```
